128 devices in a mesh: group: 2 (over x_lo), lane: 64 (over x_hi, y, z, core).
Axes of the slice: x: 4 (x_hi: 2, x_lo: 2; x = x_hi * 2 + x_lo), y: 4, z: 4, core: 2. Of those that a mesh axis runs over, the one named last changes fastest.
Arguments:
- queries: bfloat16 [8, 768], replicated, may hold values from -6 to 6
- hyper_weight: bfloat16 [768, 589824], P(None, ('group', 'lane')), may hold values from -0.0078125 to 0.0078125
- hyper_bias: bfloat16 [768, 768], P(None, ('group', 'lane')), may hold values from -0.21875 to 0.21875
- documents: bfloat16 [65536, 768], P(('group', 'lane')), may hold values from -6 to 6
- teacher: bfloat16 [65536, 8], P(('group', 'lane')), may hold values from 8 to 24
Outputs:
- doc_grad: bfloat16 [65536, 768], P(('group', 'lane'))
- weight_grad: bfloat16 [768, 589824], P(None, ('group', 'lane'))
- bias_grad: bfloat16 [768, 768], P(None, ('group', 'lane'))
The draws below stay inside these ranges and needn't reach their ends.
All inputs are finite; a program needn't handle non-finite values.
Results may differ from the reference program's by a relative error of at most 0.024.
The reference program's roundings to bfloat16 on the way count: a program that leaves them out, or rounds other values in their place, can miss the bound.
Values may be sent and summed in bfloat16 or wider, within the bound.
No kernel may reach another device: no remote copies, remote signals or barrier semaphores. Data moves between devices by JAX's collectives and lax.ppermute only.
A program may use at most 192 MiB of HBM per device.

```python
import jax
import jax.numpy as jnp
from jax import lax

D = 768
QUERIES = 8
DOCS = 65536


def level_of(rng, extent, split, least, top_value):
    def one(dim, shards_of):
        draws = jax.random.uniform(jax.random.fold_in(jax.random.fold_in(rng, 6), dim), (shards_of,), jnp.float32, least / len(split), top_value / len(split))
        return jnp.repeat(jnp.exp(draws), extent[dim] // shards_of).reshape((-1,) + (1,) * (len(extent) - dim - 1))

    factor_of = one(*split[0])
    for cut in split[1:]:
        factor_of = factor_of * one(*cut)
    return factor_of


def scatter_about(key, shape, spread, limit, split=(), held_as=jnp.bfloat16):
    level = level_of(key, shape, split, -0.22, 0.18) if split else 1.0
    drawn = jax.random.normal(key, shape, jnp.float32) * spread * level
    return jnp.minimum(jnp.maximum(drawn, -limit), limit).astype(held_as)


def setup_inputs(seed: int = 0) -> dict:
    key_of = jax.random.split(jax.random.key(seed), 6)
    return {
        "queries": scatter_about(key_of[0], (QUERIES, D), 1.0, 6.0),
        "hyper_weight": scatter_about(key_of[1], (D, D * D), (D * D) ** -0.5, 0.0078125, ((1, 128),)),
        "hyper_bias": scatter_about(key_of[2], (D, D), D ** -0.5, 0.21875, ((1, 128),)),
        "documents": scatter_about(key_of[3], (DOCS, D), 1.0, 6.0, ((0, 128),)),
        "teacher": jnp.clip(8.0 + 16.0 * jax.random.uniform(key_of[4], (DOCS, QUERIES), jnp.float32) ** level_of(key_of[4], (DOCS, QUERIES), ((0, 128),), -0.2, 0.2), 8.0, 24.0).astype(jnp.bfloat16),
    }


def reference(queries, hyper_weight, hyper_bias, documents, teacher):
    pool_scale = D ** -0.5
    query_count = queries.shape[0]
    generated = jnp.dot(queries, hyper_weight, preferred_element_type=jnp.float32).astype(jnp.bfloat16).reshape(query_count, D, D)
    gen_bias = jnp.dot(queries, hyper_bias, preferred_element_type=jnp.float32).astype(jnp.bfloat16)
    doc_float = documents.astype(jnp.float32)

    def one_query(doc_total, inputs):
        layer, bias, target = inputs
        layer_float = layer.astype(jnp.float32)
        preact = jnp.dot(doc_float, layer_float, precision=lax.Precision.HIGHEST) + bias.astype(jnp.float32)
        scores = jnp.sum(jnp.maximum(preact, 0.0), axis=1) * pool_scale
        errors = scores - target.astype(jnp.float32)
        back_pre = jnp.where(preact > 0, errors[:, None] * pool_scale, 0.0).astype(jnp.bfloat16)
        back_pre = lax.optimization_barrier(back_pre).astype(jnp.float32)
        layer_grad = jnp.dot(doc_float.T, back_pre, precision=lax.Precision.HIGHEST)
        bias_part = jnp.sum(back_pre, axis=0)
        doc_total = doc_total + jnp.dot(back_pre, layer_float.T, precision=lax.Precision.HIGHEST)
        return doc_total, (layer_grad, bias_part)

    doc_grad, (layer_grads, bias_parts) = lax.scan(one_query, jnp.zeros(doc_float.shape, jnp.float32), (generated, gen_bias, teacher.T))
    layer_grads = layer_grads.astype(jnp.bfloat16).reshape(query_count, D * D)
    bias_parts = bias_parts.astype(jnp.bfloat16)
    weight_grad = jnp.dot(queries.T, layer_grads, preferred_element_type=jnp.float32).astype(jnp.bfloat16)
    bias_grad = jnp.dot(queries.T, bias_parts, preferred_element_type=jnp.float32).astype(jnp.bfloat16)
    return doc_grad.astype(jnp.bfloat16), weight_grad, bias_grad
```

```python
import jax
import jax.numpy as jnp
from jax import lax
from jax.experimental import pallas as pl
from jax.experimental.pallas import tpu as pltpu
from jax.sharding import Mesh
from jax.sharding import PartitionSpec as P

AXES = ("xl", "xh", "y", "z", "c")
PLANE = ("xl", "xh", "y")
RING = ("z", "c")
D = 768
Q = 8
ROWS = 6
CHIPS = 16
CHUNK = 48
DOCS = 512
WIRE = 304
SCALE = D ** (-0.5)
F32 = jnp.float32
BF16 = jnp.bfloat16
TN = (((0,), (0,)), ((), ()))
NT = (((1,), (1,)), ((), ()))
NN = (((1,), (0,)), ((), ()))


def iota(shape, dim):
    return lax.broadcasted_iota(jnp.int32, shape, dim)


def one_hot(cond):
    return jnp.where(cond, 1.0, 0.0).astype(BF16)


def mm(a, b, dims=NN):
    return lax.dot_general(a, b, dims, preferred_element_type=F32)


def gen_kernel(q_ref, w_ref, hb_ref, t_ref, out_ref, qrep, acc):
    step = pl.program_id(0)
    row = iota((64, Q), 0)
    col = iota((64, Q), 1)
    sub = iota((64, D), 0) % 8

    @pl.when(step == 0)
    def _():
        rep = mm(one_hot(row // 8 == col), q_ref[...])
        qrep[...] = rep.astype(BF16)
        acc[...] = jnp.zeros_like(acc)
        placed = jnp.where(sub == 6, rep, 0.0).astype(BF16)
        acc[:, 0:ROWS] = mm(placed, hb_ref[...], NT)
        acc[:, 0:DOCS] += mm(one_hot(row == col * 8 + 7), t_ref[...])

    q = qrep[...].astype(F32)
    acc[...] += mm(jnp.where(sub == step, q, 0.0).astype(BF16), w_ref[...])

    @pl.when(step == ROWS - 1)
    def _():
        out_ref[...] = acc[...].astype(BF16)


def generate(queries, weight, bias_t, teacher_t):
    return pl.pallas_call(
        gen_kernel,
        grid=(ROWS,),
        in_specs=[
            pl.BlockSpec((Q, D), lambda i: (0, 0)),
            pl.BlockSpec((D, D), lambda i: (0, i)),
            pl.BlockSpec((ROWS, D), lambda i: (0, 0)),
            pl.BlockSpec((Q, DOCS), lambda i: (0, 0)),
        ],
        out_specs=pl.BlockSpec((64, D), lambda i: (0, 0)),
        out_shape=jax.ShapeDtypeStruct((64, D), BF16),
        scratch_shapes=[pltpu.VMEM((64, D), BF16), pltpu.VMEM((64, D), F32)],
        compiler_params=pltpu.CompilerParams(dimension_semantics=("arbitrary",)),
        cost_estimate=pl.CostEstimate(flops=2 * 64 * D * D * 6, bytes_accessed=D * D * 12, transcendentals=0),
        name="generate",
    )(queries, weight, bias_t, teacher_t)


def assemble_kernel(src_ref, r_ref, out_ref, tgt_ref):
    r = r_ref[...]
    a, b = iota((CHUNK, 64), 0), iota((CHUNK, 64), 1)
    rows = mm(one_hot((a // 6 == b // 8) & (a % 6 == b % 8)), r).astype(BF16)
    row, lane = iota((64, 128), 0), iota((64, 128), 1)
    l, m = iota((128, 128), 0), iota((128, 128), 1)
    spread = mm(r[:, 0:128], one_hot((m % 6 == l) & (l < 6) & (m < CHUNK)))
    spread = jnp.where((lane // 6 == row // 8) & (row % 8 == 6), spread, 0.0)
    bias = jnp.sum(spread, axis=0, keepdims=True)
    bias = jnp.where(iota((16, 128), 0) == 0, bias, 0.0).astype(BF16)
    for chip in range(CHIPS):
        for rb in range(3):
            for cb in range(6):
                out_ref[chip, (rb * 6 + cb) * 16 : (rb * 6 + cb + 1) * 16, :] = rows[
                    rb * 16 : (rb + 1) * 16, cb * 128 : (cb + 1) * 128
                ]
        out_ref[chip, 288:304, :] = bias
    row8, col8 = iota((64, 8), 0), iota((64, 8), 1)
    pick = jnp.zeros((64, 8), F32)
    for k in range(8):
        pick = jnp.where((col8 == k) & (row8 == src_ref[k] * 8 + 7), 1.0, pick)
    tgt_ref[...] = mm(r[:, 0:DOCS], pick.astype(BF16), TN)


def assemble(src, received):
    return pl.pallas_call(
        assemble_kernel,
        in_specs=[pl.BlockSpec(memory_space=pltpu.SMEM), pl.BlockSpec(memory_space=pltpu.VMEM)],
        out_specs=[pl.BlockSpec(memory_space=pltpu.VMEM)] * 2,
        out_shape=[
            jax.ShapeDtypeStruct((CHIPS, WIRE, 128), BF16),
            jax.ShapeDtypeStruct((DOCS, 8), F32),
        ],
        name="assemble",
    )(src, received)


def main_kernel(tgt_ref, g_ref, *refs):
    docs, outs = refs[:10], refs[10:18]
    lg_ref, dbuf, pbuf, bbuf, layer, acc, bacc, in_sem, out_sem = refs[18:]
    half = DOCS // 2
    copies = []
    for k in range(2):
        for h in range(2):
            copies.append(
                pltpu.make_async_copy(
                    docs[2 * k + h], dbuf.at[k, h * half : (h + 1) * half], in_sem.at[2 * k + h]
                )
            )
    for k in range(2, 8):
        copies.append(pltpu.make_async_copy(docs[k + 2], dbuf.at[k], in_sem.at[k + 2]))
    for copy in copies:
        copy.start()

    for chip in range(CHIPS):
        for rb in range(3):
            for cb in range(6):
                layer[
                    chip * CHUNK + rb * 16 : chip * CHUNK + (rb + 1) * 16, cb * 128 : (cb + 1) * 128
                ] = g_ref[chip, (rb * 6 + cb) * 16 : (rb * 6 + cb + 1) * 16, :]
    acc[...] = jnp.zeros_like(acc)
    bacc[...] = jnp.zeros_like(bacc)
    chip_row = iota((CHIPS, 128), 0)
    pieces = jnp.zeros((CHIPS, 128), F32)
    for chip in range(CHIPS):
        piece = g_ref[chip, 288:304, :].astype(F32)[0:1, :]
        pieces = jnp.where(chip_row == chip, piece, pieces)
    l, j = iota((128, D), 0), iota((128, D), 1)
    spread = mm(pieces.astype(BF16), one_hot((j % CHUNK == l) & (l < CHUNK)))
    own = iota((CHIPS, D), 1) // CHUNK == iota((CHIPS, D), 0)
    bias = jnp.sum(jnp.where(own, spread, 0.0), axis=0, keepdims=True)

    def block(k, carry):
        for n in range(10):

            @pl.when(k == (n // 2 if n < 4 else n - 2))
            def _():
                copies[n].wait()

        tgt = jnp.sum(
            jnp.where(iota((DOCS, 8), 1) == k, tgt_ref[...], 0.0), axis=1, keepdims=True
        )
        for h in range(2):
            rows = slice(h * half, (h + 1) * half)
            preact = mm(dbuf[k, rows], layer[...]) + bias
            scores = jnp.sum(jnp.maximum(preact, 0.0), axis=1, keepdims=True) * SCALE
            errors = (scores - tgt[rows]) * SCALE
            back = jnp.where(preact > 0, errors, 0.0).astype(BF16)
            bbuf[rows, :] = back
            bacc[...] += jnp.sum(back.astype(F32).reshape(-1, 8, D), axis=0)
        pbuf[k] = mm(bbuf[...], layer[...], NT).astype(BF16)
        for n in range(8):

            @pl.when(k == n)
            def _():
                pltpu.make_async_copy(pbuf.at[n], outs[n], out_sem.at[n]).start()

        acc[...] += mm(dbuf[k], bbuf[...], TN)
        return carry

    lax.fori_loop(0, 8, block, 0)

    for chip in range(CHIPS):
        for rb in range(3):
            rows = slice(chip * CHUNK + rb * 16, chip * CHUNK + (rb + 1) * 16)
            for cb in range(6):
                lg_ref[chip, (rb * 6 + cb) * 16 : (rb * 6 + cb + 1) * 16, :] = acc[
                    rows, cb * 128 : (cb + 1) * 128
                ].astype(BF16)
    total = jnp.sum(bacc[...], axis=0, keepdims=True)
    high = total.astype(BF16)
    low = (total - high.astype(F32)).astype(BF16)
    j, l = iota((D, 128), 0), iota((D, 128), 1)
    fold = one_hot((j % CHUNK == l) & (l < CHUNK))
    high = mm(jnp.where(own, high.astype(F32), 0.0).astype(BF16), fold)
    low = mm(jnp.where(own, low.astype(F32), 0.0).astype(BF16), fold)
    sub = iota((16, 128), 0)
    for chip in range(CHIPS):
        tile = jnp.where(sub == 0, high[chip : chip + 1], jnp.where(sub == 1, low[chip : chip + 1], 0.0))
        lg_ref[chip, 288:304, :] = tile.astype(BF16)
    for n in range(8):
        pltpu.make_async_copy(pbuf.at[n], outs[n], out_sem.at[n]).wait()


def gradients(tgt, gathered, docs):
    hbm = pl.BlockSpec(memory_space=pl.ANY)
    vmem = pl.BlockSpec(memory_space=pltpu.VMEM)
    return pl.pallas_call(
        main_kernel,
        in_specs=[vmem, vmem] + [hbm] * 10,
        out_specs=[hbm] * 8 + [vmem],
        out_shape=[jax.ShapeDtypeStruct((DOCS, D), BF16)] * 8
        + [jax.ShapeDtypeStruct((CHIPS, WIRE, 128), BF16)],
        scratch_shapes=[
            pltpu.VMEM((8, DOCS, D), BF16),
            pltpu.VMEM((8, DOCS, D), BF16),
            pltpu.VMEM((DOCS, D), BF16),
            pltpu.VMEM((D, D), BF16),
            pltpu.VMEM((D, D), F32),
            pltpu.VMEM((8, D), F32),
            pltpu.SemaphoreType.DMA((10,)),
            pltpu.SemaphoreType.DMA((8,)),
        ],
        compiler_params=pltpu.CompilerParams(vmem_limit_bytes=40 << 20),
        cost_estimate=pl.CostEstimate(
            flops=6 * 8 * DOCS * D * D, bytes_accessed=32 * DOCS * D, transcendentals=0
        ),
        name="gradients",
    )(tgt, gathered, *docs)


def reduce_kernel(y_ref, out_ref):
    total = y_ref[0].astype(F32)
    for chip in range(1, CHIPS):
        total = total + y_ref[chip].astype(F32)
    rows = jnp.concatenate(
        [
            jnp.concatenate(
                [total[(rb * 6 + cb) * 16 : (rb * 6 + cb + 1) * 16] for cb in range(6)], axis=1
            )
            for rb in range(3)
        ],
        axis=0,
    ).astype(BF16)
    a, b = iota((64, CHUNK), 0), iota((64, CHUNK), 1)
    pieces = mm(one_hot((b // 6 == a // 8) & (b % 6 == a % 8)), rows)
    bias = jnp.sum(total[288:304], axis=0, keepdims=True).astype(BF16).astype(F32)
    row, lane = iota((64, 128), 0), iota((64, 128), 1)
    mine = jnp.where((lane // 6 == row // 8) & (row % 8 == 6) & (lane < CHUNK), bias, 0.0)
    m, l = iota((128, 128), 0), iota((128, 128), 1)
    bias = mm(mine.astype(BF16), one_hot((m % 6 == l) & (l < 6) & (m < CHUNK)))
    out_ref[:, 0:128] = (pieces[:, 0:128] + bias).astype(BF16)
    out_ref[:, 128:] = pieces[:, 128:].astype(BF16)


def reduced(arrived):
    return pl.pallas_call(
        reduce_kernel,
        out_shape=jax.ShapeDtypeStruct((64, D), BF16),
        name="reduced",
    )(arrived)


def weight_kernel(q_ref, r_ref, out_ref, bias_ref, qrep):
    step = pl.program_id(0)
    row, col = iota((64, Q), 0), iota((64, Q), 1)
    sub = iota((64, D), 0) % 8

    @pl.when(step == 0)
    def _():
        rep = mm(one_hot(row // 8 == col), q_ref[...])
        qrep[...] = rep.astype(BF16)
        placed = jnp.where(sub == 6, rep, 0.0).astype(BF16)
        bias_ref[...] = mm(r_ref[:, 0:128], placed, TN)[0:8].astype(BF16)

    q = jnp.where(sub == step, qrep[...].astype(F32), 0.0).astype(BF16)
    out_ref[...] = mm(q, r_ref[...], TN).astype(BF16)


def weight_gradients(queries, received):
    return pl.pallas_call(
        weight_kernel,
        grid=(ROWS,),
        in_specs=[
            pl.BlockSpec((Q, D), lambda i: (0, 0)),
            pl.BlockSpec((64, D), lambda i: (0, 0)),
        ],
        out_specs=[
            pl.BlockSpec((D, D), lambda i: (0, i)),
            pl.BlockSpec((8, D), lambda i: (0, 0)),
        ],
        out_shape=[
            jax.ShapeDtypeStruct((D, ROWS * D), BF16),
            jax.ShapeDtypeStruct((8, D), BF16),
        ],
        scratch_shapes=[pltpu.VMEM((64, D), BF16)],
        compiler_params=pltpu.CompilerParams(dimension_semantics=("arbitrary",)),
        cost_estimate=pl.CostEstimate(flops=2 * 64 * D * D * 6, bytes_accessed=D * D * 12, transcendentals=0),
        name="weight_gradients",
    )(queries, received)


def up(a):
    return lax.ppermute(a, "z", [(i, (i + 1) % 4) for i in range(4)])


def down(a):
    return lax.ppermute(a, "z", [(i, (i + 3) % 4) for i in range(4)])


def swap(a):
    return lax.ppermute(a, "c", [(0, 1), (1, 0)])


def exchange(a, axes):
    return lax.all_to_all(a, axes, split_axis=0, concat_axis=0, tiled=True)


def add(*arrays):
    return sum(a.astype(F32) for a in arrays).astype(BF16)


def shards(queries, hyper_weight, hyper_bias, documents, teacher):
    half = DOCS // 2
    z, c = lax.axis_index("z"), lax.axis_index("c")
    below, above = up(documents), down(documents)
    far = (up(below[:half]), down(above[half:]))
    docs = [far[0], far[1], swap(far[0]), swap(far[1])]
    for mine in (below, above, documents):
        docs += [mine, swap(mine)]
    pieces = exchange(generate(queries, hyper_weight, hyper_bias.T, teacher.T), RING)
    src = jnp.stack(
        [((z + dz) % 4) * 2 + core for dz in (2, 3, 1, 0) for core in (c, 1 - c)]
    ).astype(jnp.int32)
    chunk, targets = assemble(src, pieces)
    gathered = exchange(chunk, PLANE)
    *parts, layer_grad = gradients(targets, gathered, docs)
    pieces = exchange(reduced(exchange(layer_grad, PLANE)), RING)
    weight_grad, bias_grad = weight_gradients(queries, pieces)
    far, below, above, own = parts[0::2]
    for_far, for_below, for_above, for_own = (swap(a) for a in parts[1::2])
    from_below = up(add(far[:half], for_far[:half]))
    from_above = down(add(far[half:], for_far[half:]))
    to_above = jnp.concatenate(
        [add(above[:half], for_above[:half], from_below), add(above[half:], for_above[half:])]
    )
    to_below = jnp.concatenate(
        [add(below[:half], for_below[:half]), add(below[half:], for_below[half:], from_above)]
    )
    doc_grad = add(own, for_own, up(to_above), down(to_below))
    return doc_grad, weight_grad, bias_grad[:ROWS].T


def solution(mesh):
    torus = Mesh(mesh.devices.reshape(2, 2, 4, 4, 2), AXES)
    in_specs = (P(), P(None, AXES), P(None, AXES), P(AXES, None), P(AXES, None))
    out_specs = (P(AXES, None), P(None, AXES), P(None, AXES))
    return jax.shard_map(
        shards, mesh=torus, in_specs=in_specs, out_specs=out_specs, check_vma=False
    )
```

```python
import jax
import jax.numpy as jnp
from jax import lax
from jax.experimental import pallas as pl
from jax.experimental.pallas import tpu as pltpu
from jax.sharding import Mesh
from jax.sharding import PartitionSpec as P


AXES = ("xl", "xh", "y", "z", "c")
PLANE = ("xl", "xh", "y")
RING = ("z", "c")
D = 768
Q = 8
ROWS = 6
CHIPS = 16
CHUNK = 48
DOCS = 512
WIRE = 304
TALL = 128
SCALE = D ** (-0.5)
F32 = jnp.float32
BF16 = jnp.bfloat16
TN = (((0,), (0,)), ((), ()))
NT = (((1,), (1,)), ((), ()))
NN = (((1,), (0,)), ((), ()))


def iota(shape, dim):
    return lax.broadcasted_iota(jnp.int32, shape, dim)


def one_hot(cond):
    return jnp.where(cond, 1.0, 0.0).astype(BF16)


def mm(a, b, dims=NN):
    return lax.dot_general(a, b, dims, preferred_element_type=F32)


def gen_kernel(q_ref, w_ref, hb_ref, t_ref, out_ref, qrep, acc):
    step = pl.program_id(0)
    row = iota((64, Q), 0)
    col = iota((64, Q), 1)
    sub = iota((64, D), 0) % 8

    @pl.when(step == 0)
    def _():
        rep = mm(one_hot(row // 8 == col), q_ref[...])
        qrep[...] = rep.astype(BF16)
        acc[...] = jnp.zeros_like(acc)
        placed = jnp.where(sub == 6, rep, 0.0).astype(BF16)
        acc[:, 0:ROWS] = mm(placed, hb_ref[...], NT)
        acc[:, 0:DOCS] += mm(one_hot(row == col * 8 + 7), t_ref[...])

    q = qrep[...].astype(F32)
    for n in range(2):
        placed = jnp.where(sub == step * 2 + n, q, 0.0).astype(BF16)
        acc[...] += mm(placed, w_ref[:, n * D : (n + 1) * D])

    @pl.when(step == ROWS // 2 - 1)
    def _():
        out_ref[...] = acc[...].astype(BF16)


def generate(queries, weight, bias_t, teacher_t):
    return pl.pallas_call(
        gen_kernel,
        grid=(ROWS // 2,),
        in_specs=[
            pl.BlockSpec((Q, D), lambda i: (0, 0)),
            pl.BlockSpec((D, 2 * D), lambda i: (0, i)),
            pl.BlockSpec((ROWS, D), lambda i: (0, 0)),
            pl.BlockSpec((Q, DOCS), lambda i: (0, 0)),
        ],
        out_specs=pl.BlockSpec((64, D), lambda i: (0, 0)),
        out_shape=jax.ShapeDtypeStruct((64, D), BF16),
        scratch_shapes=[pltpu.VMEM((64, D), BF16), pltpu.VMEM((64, D), F32)],
        compiler_params=pltpu.CompilerParams(dimension_semantics=("arbitrary",)),
        cost_estimate=pl.CostEstimate(flops=2 * 64 * D * D * 6, bytes_accessed=D * D * 12, transcendentals=0),
        name="generate",
    )(queries, weight, bias_t, teacher_t)


def assemble_kernel(src_ref, r_ref, out_ref, tgt_ref):
    r = r_ref[...]
    a, b = iota((CHUNK, 64), 0), iota((CHUNK, 64), 1)
    rows = mm(one_hot((a // 6 == b // 8) & (a % 6 == b % 8)), r).astype(BF16)
    row, lane = iota((64, 128), 0), iota((64, 128), 1)
    l, m = iota((128, 128), 0), iota((128, 128), 1)
    spread = mm(r[:, 0:128], one_hot((m % 6 == l) & (l < 6) & (m < CHUNK)))
    spread = jnp.where((lane // 6 == row // 8) & (row % 8 == 6), spread, 0.0)
    bias = jnp.sum(spread, axis=0, keepdims=True)
    bias = jnp.where(iota((16, 128), 0) == 0, bias, 0.0).astype(BF16)
    for chip in range(CHIPS):
        for rb in range(3):
            for cb in range(6):
                out_ref[chip, (rb * 6 + cb) * 16 : (rb * 6 + cb + 1) * 16, :] = rows[
                    rb * 16 : (rb + 1) * 16, cb * 128 : (cb + 1) * 128
                ]
        out_ref[chip, 288:304, :] = bias
    row8, col8 = iota((64, 8), 0), iota((64, 8), 1)
    pick = jnp.zeros((64, 8), F32)
    for k in range(8):
        pick = jnp.where((col8 == k) & (row8 == src_ref[k] * 8 + 7), 1.0, pick)
    tgt_ref[...] = mm(r[:, 0:DOCS], pick.astype(BF16), TN)


def assemble(src, received):
    return pl.pallas_call(
        assemble_kernel,
        in_specs=[pl.BlockSpec(memory_space=pltpu.SMEM), pl.BlockSpec(memory_space=pltpu.VMEM)],
        out_specs=[pl.BlockSpec(memory_space=pltpu.VMEM)] * 2,
        out_shape=[
            jax.ShapeDtypeStruct((CHIPS, WIRE, 128), BF16),
            jax.ShapeDtypeStruct((DOCS, 8), F32),
        ],
        name="assemble",
    )(src, received)


def main_kernel(tgt_ref, g_ref, *refs):
    docs, outs = refs[:10], refs[10:18]
    lg_ref, dbuf, bbuf, pbuf, layer, bacc, even, odd, in_sem, out_sem = refs[18:]
    half = DOCS // 2

    def block(n, size=DOCS):
        return pl.ds(n * size, size)

    for n in range(4):
        pltpu.make_async_copy(docs[n], dbuf.at[block(n, half)], in_sem.at[n // 2]).start()
    for n in range(2, 8):
        pltpu.make_async_copy(docs[n + 2], dbuf.at[block(n)], in_sem.at[n]).start()

    for chip in range(CHIPS):
        for rb in range(3):
            for cb in range(6):
                layer[
                    chip * CHUNK + rb * 16 : chip * CHUNK + (rb + 1) * 16, cb * 128 : (cb + 1) * 128
                ] = g_ref[chip, (rb * 6 + cb) * 16 : (rb * 6 + cb + 1) * 16, :]
    bacc[...] = jnp.zeros_like(bacc)
    chip_row = iota((CHIPS, 128), 0)
    pieces = jnp.zeros((CHIPS, 128), F32)
    for chip in range(CHIPS):
        piece = g_ref[chip, 288:304, :].astype(F32)[0:1, :]
        pieces = jnp.where(chip_row == chip, piece, pieces)
    l, j = iota((128, D), 0), iota((128, D), 1)
    spread = mm(pieces.astype(BF16), one_hot((j % CHUNK == l) & (l < CHUNK)))
    own = iota((CHIPS, D), 1) // CHUNK == iota((CHIPS, D), 0)
    bias = jnp.sum(jnp.where(own, spread, 0.0), axis=0, keepdims=True)

    steps = 8 * DOCS // half
    slots = (even, odd)

    def product(n):
        if n % 2 == 0:
            landed = dbuf.at[block(n // 2)]
            pltpu.make_async_copy(landed, landed, in_sem.at[n // 2]).wait()
        slots[n % 2][...] = mm(dbuf[block(n, half)], layer[...]) + bias

    def errors_of(n):
        preact = slots[n % 2][...]
        tgt = tgt_ref[block(n % 2, half)]
        tgt = jnp.sum(jnp.where(iota((half, 8), 1) == n // 2, tgt, 0.0), axis=1, keepdims=True)
        scores = jnp.sum(jnp.maximum(preact, 0.0), axis=1, keepdims=True) * SCALE
        back = jnp.where(preact > 0, (scores - tgt) * SCALE, 0.0).astype(BF16)
        bbuf[block(n, half)] = back
        bacc[...] += jnp.sum(back.astype(F32).reshape(-1, 8, D), axis=0)

    product(0)
    for n in range(steps):
        if n + 1 < steps:
            product(n + 1)
        errors_of(n)

    for n in range(4):
        rows = block(n, 2 * DOCS)
        pbuf[rows] = mm(bbuf[rows], layer[...], NT).astype(BF16)
        for k in (2 * n, 2 * n + 1):
            pltpu.make_async_copy(pbuf.at[block(k)], outs[k], out_sem.at[k]).start()

    grad = mm(dbuf[...], bbuf[...], TN).astype(BF16)
    for chip in range(CHIPS):
        for rb in range(3):
            rows = slice(chip * CHUNK + rb * 16, chip * CHUNK + (rb + 1) * 16)
            for cb in range(6):
                lg_ref[chip, (rb * 6 + cb) * 16 : (rb * 6 + cb + 1) * 16, :] = grad[
                    rows, cb * 128 : (cb + 1) * 128
                ]
    total = jnp.sum(bacc[...], axis=0, keepdims=True)
    high = total.astype(BF16)
    low = (total - high.astype(F32)).astype(BF16)
    j, l = iota((D, 128), 0), iota((D, 128), 1)
    fold = one_hot((j % CHUNK == l) & (l < CHUNK))
    high = mm(jnp.where(own, high.astype(F32), 0.0).astype(BF16), fold)
    low = mm(jnp.where(own, low.astype(F32), 0.0).astype(BF16), fold)
    sub = iota((16, 128), 0)
    for chip in range(CHIPS):
        tile = jnp.where(sub == 0, high[chip : chip + 1], jnp.where(sub == 1, low[chip : chip + 1], 0.0))
        lg_ref[chip, 288:304, :] = tile.astype(BF16)
    for n in range(8):
        pltpu.make_async_copy(pbuf.at[block(n)], outs[n], out_sem.at[n]).wait()


def gradients(tgt, gathered, docs):
    hbm = pl.BlockSpec(memory_space=pl.ANY)
    vmem = pl.BlockSpec(memory_space=pltpu.VMEM)
    return pl.pallas_call(
        main_kernel,
        in_specs=[vmem, vmem] + [hbm] * 10,
        out_specs=[hbm] * 8 + [vmem],
        out_shape=[jax.ShapeDtypeStruct((DOCS, D), BF16)] * 8
        + [jax.ShapeDtypeStruct((CHIPS, WIRE, 128), BF16)],
        scratch_shapes=[pltpu.VMEM((8 * DOCS, D), BF16)] * 3
        + [
            pltpu.VMEM((D, D), BF16),
            pltpu.VMEM((8, D), F32),
            pltpu.VMEM((DOCS // 2, D), F32),
            pltpu.VMEM((DOCS // 2, D), F32),
            pltpu.SemaphoreType.DMA((8,)),
            pltpu.SemaphoreType.DMA((8,)),
        ],
        compiler_params=pltpu.CompilerParams(vmem_limit_bytes=60 << 20),
        cost_estimate=pl.CostEstimate(
            flops=6 * 8 * DOCS * D * D, bytes_accessed=32 * DOCS * D, transcendentals=0
        ),
        name="gradients",
    )(tgt, gathered, *docs)


def reduce_kernel(y_ref, out_ref):
    total = y_ref[0].astype(F32)
    for chip in range(1, CHIPS):
        total = total + y_ref[chip].astype(F32)
    rows = jnp.concatenate(
        [
            jnp.concatenate(
                [total[(rb * 6 + cb) * 16 : (rb * 6 + cb + 1) * 16] for cb in range(6)], axis=1
            )
            for rb in range(3)
        ],
        axis=0,
    ).astype(BF16)
    a, b = iota((64, CHUNK), 0), iota((64, CHUNK), 1)
    pieces = mm(one_hot((b // 6 == a // 8) & (b % 6 == a % 8)), rows)
    bias = jnp.sum(total[288:304], axis=0, keepdims=True).astype(BF16).astype(F32)
    row, lane = iota((64, 128), 0), iota((64, 128), 1)
    mine = jnp.where((lane // 6 == row // 8) & (row % 8 == 6) & (lane < CHUNK), bias, 0.0)
    m, l = iota((128, 128), 0), iota((128, 128), 1)
    bias = mm(mine.astype(BF16), one_hot((m % 6 == l) & (l < 6) & (m < CHUNK)))
    out_ref[:, 0:128] = (pieces[:, 0:128] + bias).astype(BF16)
    out_ref[:, 128:] = pieces[:, 128:].astype(BF16)


def reduced(arrived):
    return pl.pallas_call(
        reduce_kernel,
        out_shape=jax.ShapeDtypeStruct((64, D), BF16),
        name="reduced",
    )(arrived)


def weight_kernel(q_ref, r_ref, out_ref, bias_ref):
    row, col = iota((64, Q), 0), iota((64, Q), 1)
    rep = mm(one_hot(row // 8 == col), q_ref[...])
    sub = iota((64, TALL), 0) % 8
    for n in range(ROWS):
        placed = jnp.where(sub == n, rep, 0.0).astype(BF16)
        out_ref[:, n * D : (n + 1) * D] = mm(placed, r_ref[...], TN).astype(BF16)
    placed = jnp.where(sub == 6, rep, 0.0).astype(BF16)
    bias_ref[...] = mm(r_ref[:, 0:128], placed, TN)[0:ROWS].astype(BF16)


def weight_gradients(queries, received):
    return pl.pallas_call(
        weight_kernel,
        grid=(D // TALL,),
        in_specs=[
            pl.BlockSpec((Q, TALL), lambda i: (0, i)),
            pl.BlockSpec((64, D), lambda i: (0, 0)),
        ],
        out_specs=[
            pl.BlockSpec((TALL, ROWS * D), lambda i: (i, 0)),
            pl.BlockSpec((ROWS, TALL), lambda i: (0, i)),
        ],
        out_shape=[
            jax.ShapeDtypeStruct((D, ROWS * D), BF16),
            jax.ShapeDtypeStruct((ROWS, D), BF16),
        ],
        compiler_params=pltpu.CompilerParams(dimension_semantics=("arbitrary",)),
        cost_estimate=pl.CostEstimate(
            flops=2 * 64 * D * D * 6, bytes_accessed=D * D * 12, transcendentals=0
        ),
        name="weight_gradients",
    )(queries, received)


def up(a):
    return lax.ppermute(a, "z", [(i, (i + 1) % 4) for i in range(4)])


def down(a):
    return lax.ppermute(a, "z", [(i, (i + 3) % 4) for i in range(4)])


def swap(a):
    return lax.ppermute(a, "c", [(0, 1), (1, 0)])


def exchange(a, axes):
    return lax.all_to_all(a, axes, split_axis=0, concat_axis=0, tiled=True)


def add(*arrays):
    return sum(a.astype(F32) for a in arrays).astype(BF16)


def step(queries, hyper_weight, hyper_bias, documents, teacher):
    half = DOCS // 2
    z, c = lax.axis_index("z"), lax.axis_index("c")
    generated = generate(queries, hyper_weight, hyper_bias.T, teacher.T)
    documents, generated = lax.optimization_barrier((documents, generated))
    below = up(documents)
    above = down(documents)
    far = (up(below[:half]), down(above[half:]))
    docs = [far[0], far[1], swap(far[0]), swap(far[1])]
    for mine in (below, above, documents):
        docs += [mine, swap(mine)]
    pieces = exchange(generated, RING)
    src = jnp.stack(
        [((z + dz) % 4) * 2 + core for dz in (2, 3, 1, 0) for core in (c, 1 - c)]
    ).astype(jnp.int32)
    chunk, targets = assemble(src, pieces)
    gathered = exchange(chunk, PLANE)
    *parts, layer_grad = gradients(targets, gathered, docs)
    arrived = exchange(layer_grad, PLANE)
    pieces = exchange(reduced(arrived), RING)
    far, below, above, own = parts[0::2]
    for_far, for_below, for_above, for_own = (swap(a) for a in parts[1::2])
    from_below = up(add(far[:half], for_far[:half]))
    from_above = down(add(far[half:], for_far[half:]))
    to_above = jnp.concatenate(
        [add(above[:half], for_above[:half], from_below), add(above[half:], for_above[half:])]
    )
    to_below = jnp.concatenate(
        [add(below[:half], for_below[:half]), add(below[half:], for_below[half:], from_above)]
    )
    from_below = up(to_above)
    from_above = down(to_below)
    doc_grad = add(own, for_own, from_below, from_above)
    doc_grad, pieces = lax.optimization_barrier((doc_grad, pieces))
    weight_grad, bias_grad = weight_gradients(queries, pieces)
    return doc_grad, weight_grad, bias_grad.T


def solution(mesh):
    torus = Mesh(mesh.devices.reshape(2, 2, 4, 4, 2), AXES)
    in_specs = (P(), P(None, AXES), P(None, AXES), P(AXES, None), P(AXES, None))
    out_specs = (P(AXES, None), P(None, AXES), P(None, AXES))
    return jax.shard_map(step, mesh=torus, in_specs=in_specs, out_specs=out_specs, check_vma=False)
```

```python
import functools

import jax
import jax.numpy as jnp
from jax import lax
from jax.experimental import pallas as pl
from jax.experimental.pallas import tpu as pltpu
from jax.sharding import Mesh
from jax.sharding import PartitionSpec as P


AXES = ("xl", "xh", "y", "z", "c")
PLANE = ("xl", "xh", "y")
RING = ("z", "c")
D = 768
Q = 8
ROWS = 6
CHIPS = 16
CHUNK = 48
DOCS = 512
WIRE = 304
TALL = 128
SCALE = D ** (-0.5)
F32 = jnp.float32
BF16 = jnp.bfloat16
TN = (((0,), (0,)), ((), ()))
NT = (((1,), (1,)), ((), ()))
NN = (((1,), (0,)), ((), ()))


def iota(shape, dim):
    return lax.broadcasted_iota(jnp.int32, shape, dim)


def one_hot(cond):
    return jnp.where(cond, 1.0, 0.0).astype(BF16)


def mm(a, b, dims=NN):
    return lax.dot_general(a, b, dims, preferred_element_type=F32)


def gen_kernel(q_ref, w_ref, hb_ref, t_ref, out_ref, wbuf, sem):
    def columns(n):
        cols = pl.ds(n * D, D)
        return pltpu.make_async_copy(w_ref.at[:, cols], wbuf.at[:, cols], sem.at[n])

    for n in range(ROWS):
        columns(n).start()
    row, col = iota((64, Q), 0), iota((64, Q), 1)
    sub = iota((64, D), 0) % 8
    rep = mm(one_hot(row // 8 == col), q_ref[...])
    placed = jnp.where(sub == 6, rep, 0.0).astype(BF16)
    bias = mm(placed, hb_ref[...], NT)
    targets = mm(one_hot(row == col * 8 + 7), t_ref[...])
    total = jnp.zeros((64, D), F32)
    for n in range(ROWS):
        placed = jnp.where(sub == n, rep, 0.0).astype(BF16)
        columns(n).wait()
        total = total + mm(placed, wbuf[:, n * D : (n + 1) * D])
    out_ref[:, DOCS:] = total[:, DOCS:].astype(BF16)
    total = total[:, 0:DOCS] + targets
    out_ref[:, 128:DOCS] = total[:, 128:].astype(BF16)
    m, l = iota((8, 128), 0), iota((8, 128), 1)
    bias = jnp.concatenate([bias, jnp.zeros((64, 2), F32)], axis=1).astype(BF16)
    bias = mm(bias, one_hot(m == l))
    out_ref[:, 0:128] = (total[:, 0:128] + bias).astype(BF16)


def generate(queries, weight, bias_t, teacher_t):
    vmem = pl.BlockSpec(memory_space=pltpu.VMEM)
    return pl.pallas_call(
        gen_kernel,
        in_specs=[vmem, pl.BlockSpec(memory_space=pl.ANY), vmem, vmem],
        out_specs=vmem,
        out_shape=jax.ShapeDtypeStruct((64, D), BF16),
        scratch_shapes=[pltpu.VMEM((D, ROWS * D), BF16), pltpu.SemaphoreType.DMA((ROWS,))],
        compiler_params=pltpu.CompilerParams(vmem_limit_bytes=60 << 20),
        cost_estimate=pl.CostEstimate(
            flops=2 * 64 * D * D * 6, bytes_accessed=D * D * 12, transcendentals=0
        ),
        name="generate",
    )(queries, weight, bias_t, teacher_t)


def assemble_kernel(src_ref, r_ref, out_ref, tgt_ref):
    r = r_ref[...]
    a, b = iota((CHUNK, 64), 0), iota((CHUNK, 64), 1)
    rows = mm(one_hot((a // 6 == b // 8) & (a % 6 == b % 8)), r).astype(BF16)
    row, lane = iota((64, 128), 0), iota((64, 128), 1)
    l, m = iota((128, 128), 0), iota((128, 128), 1)
    spread = mm(r[:, 0:128], one_hot((m % 6 == l) & (l < 6) & (m < CHUNK)))
    spread = jnp.where((lane // 6 == row // 8) & (row % 8 == 6), spread, 0.0)
    bias = jnp.sum(spread, axis=0, keepdims=True)
    bias = jnp.where(iota((16, 128), 0) == 0, bias, 0.0).astype(BF16)
    for chip in range(CHIPS):
        for rb in range(3):
            for cb in range(6):
                out_ref[chip, (rb * 6 + cb) * 16 : (rb * 6 + cb + 1) * 16, :] = rows[
                    rb * 16 : (rb + 1) * 16, cb * 128 : (cb + 1) * 128
                ]
        out_ref[chip, 288:304, :] = bias
    row8, col8 = iota((64, 8), 0), iota((64, 8), 1)
    pick = jnp.zeros((64, 8), F32)
    for k in range(8):
        pick = jnp.where((col8 == k) & (row8 == src_ref[k] * 8 + 7), 1.0, pick)
    tgt_ref[...] = mm(r[:, 0:DOCS], pick.astype(BF16), TN)


def assemble(src, received):
    return pl.pallas_call(
        assemble_kernel,
        in_specs=[pl.BlockSpec(memory_space=pltpu.SMEM), pl.BlockSpec(memory_space=pltpu.VMEM)],
        out_specs=[pl.BlockSpec(memory_space=pltpu.VMEM)] * 2,
        out_shape=[
            jax.ShapeDtypeStruct((CHIPS, WIRE, 128), BF16),
            jax.ShapeDtypeStruct((DOCS, 8), F32),
        ],
        compiler_params=pltpu.CompilerParams(vmem_limit_bytes=8 << 20),
        name="assemble",
    )(src, received)


def main_kernel(tgt_ref, g_ref, *refs):
    docs, outs = refs[:14], refs[14:22]
    lg_ref, dbuf, bbuf, pbuf, layer, bacc, even, odd, in_sem, out_sem = refs[22:]
    half = DOCS // 2

    def block(n, size=DOCS):
        return pl.ds(n * size, size)

    for n in range(12):
        pltpu.make_async_copy(docs[n], dbuf.at[block(n, half)], in_sem.at[n // 2]).start()
    for n in range(6, 8):
        pltpu.make_async_copy(docs[n + 6], dbuf.at[block(n)], in_sem.at[n]).start()

    for chip in range(CHIPS):
        for rb in range(3):
            for cb in range(6):
                layer[
                    chip * CHUNK + rb * 16 : chip * CHUNK + (rb + 1) * 16, cb * 128 : (cb + 1) * 128
                ] = g_ref[chip, (rb * 6 + cb) * 16 : (rb * 6 + cb + 1) * 16, :]
    bacc[...] = jnp.zeros_like(bacc)
    chip_row = iota((CHIPS, 128), 0)
    pieces = jnp.zeros((CHIPS, 128), F32)
    for chip in range(CHIPS):
        piece = g_ref[chip, 288:304, :].astype(F32)[0:1, :]
        pieces = jnp.where(chip_row == chip, piece, pieces)
    l, j = iota((128, D), 0), iota((128, D), 1)
    spread = mm(pieces.astype(BF16), one_hot((j % CHUNK == l) & (l < CHUNK)))
    own = iota((CHIPS, D), 1) // CHUNK == iota((CHIPS, D), 0)
    bias = jnp.sum(jnp.where(own, spread, 0.0), axis=0, keepdims=True)

    steps = 8 * DOCS // half
    slots = (even, odd)

    def product(n):
        if n % 2 == 0:
            landed = dbuf.at[block(n // 2)]
            pltpu.make_async_copy(landed, landed, in_sem.at[n // 2]).wait()
        slots[n % 2][...] = mm(dbuf[block(n, half)], layer[...]) + bias

    def errors_of(n):
        preact = slots[n % 2][...]
        tgt = tgt_ref[block(n % 2, half)]
        tgt = jnp.sum(jnp.where(iota((half, 8), 1) == n // 2, tgt, 0.0), axis=1, keepdims=True)
        scores = jnp.sum(jnp.maximum(preact, 0.0), axis=1, keepdims=True) * SCALE
        back = jnp.where(preact > 0, (scores - tgt) * SCALE, 0.0).astype(BF16)
        bbuf[block(n, half)] = back
        bacc[...] += jnp.sum(back.astype(F32).reshape(-1, 8, D), axis=0)

    product(0)
    for n in range(steps):
        if n + 1 < steps:
            product(n + 1)
        errors_of(n)

    for n in range(4):
        rows = block(n, 2 * DOCS)
        pbuf[rows] = mm(bbuf[rows], layer[...], NT).astype(BF16)
        for k in (2 * n, 2 * n + 1):
            pltpu.make_async_copy(pbuf.at[block(k)], outs[k], out_sem.at[k]).start()

    grad = mm(dbuf[...], bbuf[...], TN).astype(BF16)
    for chip in range(CHIPS):
        for rb in range(3):
            rows = slice(chip * CHUNK + rb * 16, chip * CHUNK + (rb + 1) * 16)
            for cb in range(6):
                lg_ref[chip, (rb * 6 + cb) * 16 : (rb * 6 + cb + 1) * 16, :] = grad[
                    rows, cb * 128 : (cb + 1) * 128
                ]
    total = jnp.sum(bacc[...], axis=0, keepdims=True)
    high = total.astype(BF16)
    low = (total - high.astype(F32)).astype(BF16)
    j, l = iota((D, 128), 0), iota((D, 128), 1)
    fold = one_hot((j % CHUNK == l) & (l < CHUNK))
    high = mm(jnp.where(own, high.astype(F32), 0.0).astype(BF16), fold)
    low = mm(jnp.where(own, low.astype(F32), 0.0).astype(BF16), fold)
    sub = iota((16, 128), 0)
    for chip in range(CHIPS):
        tile = jnp.where(sub == 0, high[chip : chip + 1], jnp.where(sub == 1, low[chip : chip + 1], 0.0))
        lg_ref[chip, 288:304, :] = tile.astype(BF16)
    for n in range(8):
        pltpu.make_async_copy(pbuf.at[block(n)], outs[n], out_sem.at[n]).wait()


def gradients(tgt, gathered, docs):
    hbm = pl.BlockSpec(memory_space=pl.ANY)
    vmem = pl.BlockSpec(memory_space=pltpu.VMEM)
    return pl.pallas_call(
        main_kernel,
        in_specs=[vmem, vmem] + [hbm] * 14,
        out_specs=[hbm] * 8 + [vmem],
        out_shape=[jax.ShapeDtypeStruct((DOCS, D), BF16)] * 8
        + [jax.ShapeDtypeStruct((CHIPS, WIRE, 128), BF16)],
        scratch_shapes=[pltpu.VMEM((8 * DOCS, D), BF16)] * 3
        + [
            pltpu.VMEM((D, D), BF16),
            pltpu.VMEM((8, D), F32),
            pltpu.VMEM((DOCS // 2, D), F32),
            pltpu.VMEM((DOCS // 2, D), F32),
            pltpu.SemaphoreType.DMA((8,)),
            pltpu.SemaphoreType.DMA((8,)),
        ],
        compiler_params=pltpu.CompilerParams(vmem_limit_bytes=60 << 20),
        cost_estimate=pl.CostEstimate(
            flops=6 * 8 * DOCS * D * D, bytes_accessed=32 * DOCS * D, transcendentals=0
        ),
        name="gradients",
    )(tgt, gathered, *docs)


def reduce_kernel(y_ref, out_ref):
    total = y_ref[0].astype(F32)
    for chip in range(1, CHIPS):
        total = total + y_ref[chip].astype(F32)
    rows = jnp.concatenate(
        [
            jnp.concatenate(
                [total[(rb * 6 + cb) * 16 : (rb * 6 + cb + 1) * 16] for cb in range(6)], axis=1
            )
            for rb in range(3)
        ],
        axis=0,
    ).astype(BF16)
    a, b = iota((64, CHUNK), 0), iota((64, CHUNK), 1)
    pieces = mm(one_hot((b // 6 == a // 8) & (b % 6 == a % 8)), rows)
    bias = jnp.sum(total[288:304], axis=0, keepdims=True).astype(BF16).astype(F32)
    row, lane = iota((64, 128), 0), iota((64, 128), 1)
    mine = jnp.where((lane // 6 == row // 8) & (row % 8 == 6) & (lane < CHUNK), bias, 0.0)
    m, l = iota((128, 128), 0), iota((128, 128), 1)
    bias = mm(mine.astype(BF16), one_hot((m % 6 == l) & (l < 6) & (m < CHUNK)))
    out_ref[:, 0:128] = (pieces[:, 0:128] + bias).astype(BF16)
    out_ref[:, 128:] = pieces[:, 128:].astype(BF16)


def reduced(arrived):
    return pl.pallas_call(
        reduce_kernel,
        out_shape=jax.ShapeDtypeStruct((64, D), BF16),
        compiler_params=pltpu.CompilerParams(vmem_limit_bytes=8 << 20),
        name="reduced",
    )(arrived)


def weight_kernel(q_ref, r_ref, out_ref, bias_ref, obuf, sem):
    def rows_of(n):
        rows = pl.ds(n * TALL, TALL)
        return pltpu.make_async_copy(obuf.at[rows], out_ref.at[rows], sem.at[n])

    row, col = iota((64, Q), 0), iota((64, Q), 1)
    sub = iota((64, D), 0) % 8
    rep = mm(one_hot(row // 8 == col), q_ref[...])
    placed = [jnp.where(sub == n, rep, 0.0).astype(BF16) for n in range(7)]
    for k in range(D // TALL):
        rows = slice(k * TALL, (k + 1) * TALL)
        for n in range(ROWS):
            obuf[rows, n * D : (n + 1) * D] = mm(placed[n][:, rows], r_ref[...], TN).astype(BF16)
        rows_of(k).start()
    bias_ref[...] = mm(r_ref[:, 0:128], placed[6], TN)[0:ROWS].astype(BF16)
    for k in range(D // TALL):
        rows_of(k).wait()


def weight_gradients(queries, received):
    vmem = pl.BlockSpec(memory_space=pltpu.VMEM)
    return pl.pallas_call(
        weight_kernel,
        in_specs=[vmem, vmem],
        out_specs=[pl.BlockSpec(memory_space=pl.ANY), vmem],
        out_shape=[
            jax.ShapeDtypeStruct((D, ROWS * D), BF16),
            jax.ShapeDtypeStruct((ROWS, D), BF16),
        ],
        scratch_shapes=[
            pltpu.VMEM((D, ROWS * D), BF16),
            pltpu.SemaphoreType.DMA((D // TALL,)),
        ],
        compiler_params=pltpu.CompilerParams(vmem_limit_bytes=16 << 20),
        cost_estimate=pl.CostEstimate(
            flops=2 * 64 * D * D * 6, bytes_accessed=D * D * 12, transcendentals=0
        ),
        name="weight_gradients",
    )(queries, received)


def sums_kernel(sizes, *refs):
    outs = refs[sum(sizes) :]
    at = 0
    for out, size in zip(outs, sizes):
        total = refs[at][...].astype(F32)
        for term in refs[at + 1 : at + size]:
            total = total + term[...].astype(F32)
        out[...] = total.astype(BF16)
        at += size


def sums(*groups):
    def half_of(h):
        return pl.BlockSpec((DOCS // 4, D), lambda i: (2 * h + i, 0))

    terms = [term for group in groups for term in group]
    return pl.pallas_call(
        functools.partial(sums_kernel, [len(group) for group in groups]),
        grid=(2,),
        in_specs=[half_of(h) for _, h in terms],
        out_specs=[half_of(0) for _ in groups],
        out_shape=[jax.ShapeDtypeStruct((DOCS // 2, D), BF16) for _ in groups],
        compiler_params=pltpu.CompilerParams(vmem_limit_bytes=12 << 20),
        cost_estimate=pl.CostEstimate(
            flops=len(terms) * DOCS * D, bytes_accessed=len(terms) * DOCS * D, transcendentals=0
        ),
    )(*(array for array, _ in terms))


def final_kernel(mine_ref, other_ref, ul_ref, dl_ref, uh_ref, dh_ref, out_ref):
    half = DOCS // 2
    for rows, a, b in ((slice(0, half), ul_ref, dl_ref), (slice(half, DOCS), uh_ref, dh_ref)):
        total = mine_ref[rows].astype(F32) + other_ref[rows].astype(F32)
        total = total + a[...].astype(F32) + b[...].astype(F32)
        out_ref[rows] = total.astype(BF16)


def document_sum(*parts):
    return pl.pallas_call(
        final_kernel,
        out_shape=jax.ShapeDtypeStruct((DOCS, D), BF16),
        compiler_params=pltpu.CompilerParams(vmem_limit_bytes=12 << 20),
        cost_estimate=pl.CostEstimate(
            flops=4 * DOCS * D, bytes_accessed=10 * DOCS * D, transcendentals=0
        ),
        name="document_sum",
    )(*parts)


def up(a):
    return lax.ppermute(a, "z", [(i, (i + 1) % 4) for i in range(4)])


def down(a):
    return lax.ppermute(a, "z", [(i, (i + 3) % 4) for i in range(4)])


def swap(a):
    return lax.ppermute(a, "c", [(0, 1), (1, 0)])


def exchange(a, axes):
    return lax.all_to_all(a, axes, split_axis=0, concat_axis=0, tiled=True)


def step(queries, hyper_weight, hyper_bias, documents, teacher):
    half = DOCS // 2
    z, c = lax.axis_index("z"), lax.axis_index("c")
    generated = generate(queries, hyper_weight, hyper_bias.T, teacher.T)
    documents, generated = lax.optimization_barrier((documents, generated))
    low, high = documents[:half], documents[half:]
    below_low = up(low)
    above_high = down(high)
    below_high = up(high)
    above_low = down(low)
    far = (up(below_low), down(above_high))
    docs = []
    for pair in (far, (below_low, below_high), (above_low, above_high)):
        docs += [*pair, swap(pair[0]), swap(pair[1])]
    docs += [documents, swap(documents)]
    pieces = exchange(generated, RING)
    src = jnp.stack(
        [((z + dz) % 4) * 2 + core for dz in (2, 3, 1, 0) for core in (c, 1 - c)]
    ).astype(jnp.int32)
    chunk, targets = assemble(src, pieces)
    gathered = exchange(chunk, PLANE)
    *parts, layer_grad = gradients(targets, gathered, docs)
    arrived = exchange(layer_grad, PLANE)
    pieces = exchange(reduced(arrived), RING)
    far, below, above, own = parts[0::2]
    for_far, for_below, for_above, for_own = (swap(a) for a in parts[1::2])
    first = sums([(far, 0), (for_far, 0)], [(far, 1), (for_far, 1)])
    far_low, far_high = up(first[0]), down(first[1])
    second = sums([(above, 1), (for_above, 1)], [(below, 0), (for_below, 0)])
    up_high, down_low = up(second[0]), down(second[1])
    third = sums(
        [(above, 0), (for_above, 0), (far_low, 0)], [(below, 1), (for_below, 1), (far_high, 0)]
    )
    up_low, down_high = up(third[0]), down(third[1])
    doc_grad = document_sum(own, for_own, up_low, down_low, up_high, down_high)
    weight_grad, bias_grad = weight_gradients(queries, pieces)
    return doc_grad, weight_grad, bias_grad.T


def solution(mesh):
    torus = Mesh(mesh.devices.reshape(2, 2, 4, 4, 2), AXES)
    in_specs = (P(), P(None, AXES), P(None, AXES), P(AXES, None), P(AXES, None))
    out_specs = (P(AXES, None), P(None, AXES), P(None, AXES))
    return jax.shard_map(step, mesh=torus, in_specs=in_specs, out_specs=out_specs, check_vma=False)
```

```python
import functools

import jax
import jax.numpy as jnp
from jax import lax
from jax.experimental import pallas as pl
from jax.experimental.pallas import tpu as pltpu
from jax.sharding import Mesh
from jax.sharding import PartitionSpec as P


AXES = ("xl", "xh", "y", "z", "c")
PLANE = ("xl", "xh", "y")
RING = ("z", "c")
D = 768
Q = 8
ROWS = 6
CHIPS = 16
CHUNK = 48
DOCS = 512
WIRE = 304
TALL = 128
SCALE = D ** (-0.5)
F32 = jnp.float32
BF16 = jnp.bfloat16
TN = (((0,), (0,)), ((), ()))
NT = (((1,), (1,)), ((), ()))
NN = (((1,), (0,)), ((), ()))


def iota(shape, dim):
    return lax.broadcasted_iota(jnp.int32, shape, dim)


def one_hot(cond):
    return jnp.where(cond, 1.0, 0.0).astype(BF16)


def mm(a, b, dims=NN):
    return lax.dot_general(a, b, dims, preferred_element_type=F32)


def gen_kernel(q_ref, w_ref, hb_ref, t_ref, d_ref, out_ref, low_ref, high_ref, wbuf, dbuf, sem):
    def columns(n):
        cols = pl.ds(n * D, D)
        return pltpu.make_async_copy(w_ref.at[:, cols], wbuf.at[:, cols], sem.at[n])

    half = DOCS // 2
    docs_in = pltpu.make_async_copy(d_ref, dbuf, sem.at[ROWS])
    low_out = pltpu.make_async_copy(dbuf.at[0:half], low_ref, sem.at[ROWS + 1])
    high_out = pltpu.make_async_copy(dbuf.at[half:DOCS], high_ref, sem.at[ROWS + 2])
    for n in range(ROWS):
        columns(n).start()
        if n == 2:
            docs_in.start()
    row, col = iota((64, Q), 0), iota((64, Q), 1)
    sub = iota((64, D), 0) % 8
    rep = mm(one_hot(row // 8 == col), q_ref[...])
    placed = jnp.where(sub == 6, rep, 0.0).astype(BF16)
    bias = mm(placed, hb_ref[...], NT)
    targets = mm(one_hot(row == col * 8 + 7), t_ref[...])
    total = jnp.zeros((64, D), F32)
    for n in range(ROWS):
        placed = jnp.where(sub == n, rep, 0.0).astype(BF16)
        columns(n).wait()
        if n == ROWS - 2:
            docs_in.wait()
            low_out.start()
            high_out.start()
        total = total + mm(placed, wbuf[:, n * D : (n + 1) * D])
    out_ref[:, DOCS:] = total[:, DOCS:].astype(BF16)
    total = total[:, 0:DOCS] + targets
    out_ref[:, 128:DOCS] = total[:, 128:].astype(BF16)
    m, l = iota((8, 128), 0), iota((8, 128), 1)
    bias = jnp.concatenate([bias, jnp.zeros((64, 2), F32)], axis=1).astype(BF16)
    bias = mm(bias, one_hot(m == l))
    out_ref[:, 0:128] = (total[:, 0:128] + bias).astype(BF16)
    low_out.wait()
    high_out.wait()


def generate(queries, weight, bias_t, teacher_t, documents):
    hbm = pl.BlockSpec(memory_space=pl.ANY)
    vmem = pl.BlockSpec(memory_space=pltpu.VMEM)
    return pl.pallas_call(
        gen_kernel,
        in_specs=[vmem, hbm, vmem, vmem, hbm],
        out_specs=[vmem, hbm, hbm],
        out_shape=[jax.ShapeDtypeStruct((64, D), BF16)]
        + [jax.ShapeDtypeStruct((DOCS // 2, D), BF16)] * 2,
        scratch_shapes=[
            pltpu.VMEM((D, ROWS * D), BF16),
            pltpu.VMEM((DOCS, D), BF16),
            pltpu.SemaphoreType.DMA((ROWS + 3,)),
        ],
        compiler_params=pltpu.CompilerParams(vmem_limit_bytes=60 << 20),
        cost_estimate=pl.CostEstimate(
            flops=2 * 64 * D * D * 6, bytes_accessed=D * D * 12, transcendentals=0
        ),
        name="generate",
    )(queries, weight, bias_t, teacher_t, documents)


def assemble_kernel(src_ref, r_ref, out_ref, tgt_ref):
    r = r_ref[...]
    a, b = iota((CHUNK, 64), 0), iota((CHUNK, 64), 1)
    rows = mm(one_hot((a // 6 == b // 8) & (a % 6 == b % 8)), r).astype(BF16)
    row, lane = iota((64, 128), 0), iota((64, 128), 1)
    l, m = iota((128, 128), 0), iota((128, 128), 1)
    spread = mm(r[:, 0:128], one_hot((m % 6 == l) & (l < 6) & (m < CHUNK)))
    spread = jnp.where((lane // 6 == row // 8) & (row % 8 == 6), spread, 0.0)
    bias = jnp.sum(spread, axis=0, keepdims=True)
    bias = jnp.where(iota((16, 128), 0) == 0, bias, 0.0).astype(BF16)
    for chip in range(CHIPS):
        for rb in range(3):
            for cb in range(6):
                out_ref[chip, (rb * 6 + cb) * 16 : (rb * 6 + cb + 1) * 16, :] = rows[
                    rb * 16 : (rb + 1) * 16, cb * 128 : (cb + 1) * 128
                ]
        out_ref[chip, 288:304, :] = bias
    row8, col8 = iota((64, 8), 0), iota((64, 8), 1)
    pick = jnp.zeros((64, 8), F32)
    for k in range(8):
        pick = jnp.where((col8 == k) & (row8 == src_ref[k] * 8 + 7), 1.0, pick)
    tgt_ref[...] = mm(r[:, 0:DOCS], pick.astype(BF16), TN)


def assemble(src, received):
    return pl.pallas_call(
        assemble_kernel,
        in_specs=[pl.BlockSpec(memory_space=pltpu.SMEM), pl.BlockSpec(memory_space=pltpu.VMEM)],
        out_specs=[pl.BlockSpec(memory_space=pltpu.VMEM)] * 2,
        out_shape=[
            jax.ShapeDtypeStruct((CHIPS, WIRE, 128), BF16),
            jax.ShapeDtypeStruct((DOCS, 8), F32),
        ],
        compiler_params=pltpu.CompilerParams(vmem_limit_bytes=8 << 20),
        name="assemble",
    )(src, received)


def main_kernel(tgt_ref, g_ref, *refs):
    docs, outs = refs[:14], refs[14:22]
    lg_ref, dbuf, bbuf, pbuf, layer, bacc, even, odd, in_sem, out_sem = refs[22:]
    half = DOCS // 2

    def block(n, size=DOCS):
        return pl.ds(n * size, size)

    for n in range(12):
        pltpu.make_async_copy(docs[n], dbuf.at[block(n, half)], in_sem.at[n // 2]).start()
    for n in range(6, 8):
        pltpu.make_async_copy(docs[n + 6], dbuf.at[block(n)], in_sem.at[n]).start()

    for chip in range(CHIPS):
        for rb in range(3):
            for cb in range(6):
                layer[
                    chip * CHUNK + rb * 16 : chip * CHUNK + (rb + 1) * 16, cb * 128 : (cb + 1) * 128
                ] = g_ref[chip, (rb * 6 + cb) * 16 : (rb * 6 + cb + 1) * 16, :]
    bacc[...] = jnp.zeros_like(bacc)
    chip_row = iota((CHIPS, 128), 0)
    pieces = jnp.zeros((CHIPS, 128), F32)
    for chip in range(CHIPS):
        piece = g_ref[chip, 288:304, :].astype(F32)[0:1, :]
        pieces = jnp.where(chip_row == chip, piece, pieces)
    l, j = iota((128, D), 0), iota((128, D), 1)
    spread = mm(pieces.astype(BF16), one_hot((j % CHUNK == l) & (l < CHUNK)))
    own = iota((CHIPS, D), 1) // CHUNK == iota((CHIPS, D), 0)
    bias = jnp.sum(jnp.where(own, spread, 0.0), axis=0, keepdims=True)

    steps = 8 * DOCS // half
    slots = (even, odd)

    def product(n):
        if n % 2 == 0:
            landed = dbuf.at[block(n // 2)]
            pltpu.make_async_copy(landed, landed, in_sem.at[n // 2]).wait()
        slots[n % 2][...] = mm(dbuf[block(n, half)], layer[...]) + bias

    def errors_of(n):
        preact = slots[n % 2][...]
        tgt = tgt_ref[block(n % 2, half)]
        tgt = jnp.sum(jnp.where(iota((half, 8), 1) == n // 2, tgt, 0.0), axis=1, keepdims=True)
        scores = jnp.sum(jnp.maximum(preact, 0.0), axis=1, keepdims=True) * SCALE
        back = jnp.where(preact > 0, (scores - tgt) * SCALE, 0.0).astype(BF16)
        bbuf[block(n, half)] = back
        bacc[...] += jnp.sum(back.astype(F32).reshape(-1, 8, D), axis=0)

    product(0)
    for n in range(steps):
        if n + 1 < steps:
            product(n + 1)
        errors_of(n)

    for n in range(4):
        rows = block(n, 2 * DOCS)
        pbuf[rows] = mm(bbuf[rows], layer[...], NT).astype(BF16)
        for k in (2 * n, 2 * n + 1):
            pltpu.make_async_copy(pbuf.at[block(k)], outs[k], out_sem.at[k]).start()

    grad = mm(dbuf[...], bbuf[...], TN).astype(BF16)
    for chip in range(CHIPS):
        for rb in range(3):
            rows = slice(chip * CHUNK + rb * 16, chip * CHUNK + (rb + 1) * 16)
            for cb in range(6):
                lg_ref[chip, (rb * 6 + cb) * 16 : (rb * 6 + cb + 1) * 16, :] = grad[
                    rows, cb * 128 : (cb + 1) * 128
                ]
    total = jnp.sum(bacc[...], axis=0, keepdims=True)
    high = total.astype(BF16)
    low = (total - high.astype(F32)).astype(BF16)
    j, l = iota((D, 128), 0), iota((D, 128), 1)
    fold = one_hot((j % CHUNK == l) & (l < CHUNK))
    high = mm(jnp.where(own, high.astype(F32), 0.0).astype(BF16), fold)
    low = mm(jnp.where(own, low.astype(F32), 0.0).astype(BF16), fold)
    sub = iota((16, 128), 0)
    for chip in range(CHIPS):
        tile = jnp.where(sub == 0, high[chip : chip + 1], jnp.where(sub == 1, low[chip : chip + 1], 0.0))
        lg_ref[chip, 288:304, :] = tile.astype(BF16)
    for n in range(8):
        pltpu.make_async_copy(pbuf.at[block(n)], outs[n], out_sem.at[n]).wait()


def gradients(tgt, gathered, docs):
    hbm = pl.BlockSpec(memory_space=pl.ANY)
    vmem = pl.BlockSpec(memory_space=pltpu.VMEM)
    return pl.pallas_call(
        main_kernel,
        in_specs=[vmem, vmem] + [hbm] * 14,
        out_specs=[hbm] * 8 + [vmem],
        out_shape=[jax.ShapeDtypeStruct((DOCS, D), BF16)] * 8
        + [jax.ShapeDtypeStruct((CHIPS, WIRE, 128), BF16)],
        scratch_shapes=[pltpu.VMEM((8 * DOCS, D), BF16)] * 3
        + [
            pltpu.VMEM((D, D), BF16),
            pltpu.VMEM((8, D), F32),
            pltpu.VMEM((DOCS // 2, D), F32),
            pltpu.VMEM((DOCS // 2, D), F32),
            pltpu.SemaphoreType.DMA((8,)),
            pltpu.SemaphoreType.DMA((8,)),
        ],
        compiler_params=pltpu.CompilerParams(vmem_limit_bytes=51 << 20),
        cost_estimate=pl.CostEstimate(
            flops=6 * 8 * DOCS * D * D, bytes_accessed=32 * DOCS * D, transcendentals=0
        ),
        name="gradients",
    )(tgt, gathered, *docs)


def reduce_kernel(y_ref, out_ref):
    total = y_ref[0].astype(F32)
    for chip in range(1, CHIPS):
        total = total + y_ref[chip].astype(F32)
    rows = jnp.concatenate(
        [
            jnp.concatenate(
                [total[(rb * 6 + cb) * 16 : (rb * 6 + cb + 1) * 16] for cb in range(6)], axis=1
            )
            for rb in range(3)
        ],
        axis=0,
    ).astype(BF16)
    a, b = iota((64, CHUNK), 0), iota((64, CHUNK), 1)
    pieces = mm(one_hot((b // 6 == a // 8) & (b % 6 == a % 8)), rows)
    bias = jnp.sum(total[288:304], axis=0, keepdims=True).astype(BF16).astype(F32)
    row, lane = iota((64, 128), 0), iota((64, 128), 1)
    mine = jnp.where((lane // 6 == row // 8) & (row % 8 == 6) & (lane < CHUNK), bias, 0.0)
    m, l = iota((128, 128), 0), iota((128, 128), 1)
    bias = mm(mine.astype(BF16), one_hot((m % 6 == l) & (l < 6) & (m < CHUNK)))
    out_ref[:, 0:128] = (pieces[:, 0:128] + bias).astype(BF16)
    out_ref[:, 128:] = pieces[:, 128:].astype(BF16)


def reduced(arrived):
    return pl.pallas_call(
        reduce_kernel,
        out_shape=jax.ShapeDtypeStruct((64, D), BF16),
        compiler_params=pltpu.CompilerParams(vmem_limit_bytes=8 << 20),
        name="reduced",
    )(arrived)


def weight_kernel(q_ref, r_ref, out_ref, bias_ref, obuf, sem):
    def rows_of(n):
        rows = pl.ds(n * TALL, TALL)
        return pltpu.make_async_copy(obuf.at[rows], out_ref.at[rows], sem.at[n])

    row, col = iota((64, Q), 0), iota((64, Q), 1)
    sub = iota((64, D), 0) % 8
    rep = mm(one_hot(row // 8 == col), q_ref[...])
    placed = [jnp.where(sub == n, rep, 0.0).astype(BF16) for n in range(7)]
    for k in range(D // TALL):
        rows = slice(k * TALL, (k + 1) * TALL)
        for n in range(ROWS):
            obuf[rows, n * D : (n + 1) * D] = mm(placed[n][:, rows], r_ref[...], TN).astype(BF16)
        rows_of(k).start()
    bias_ref[...] = mm(r_ref[:, 0:128], placed[6], TN)[0:ROWS].astype(BF16)
    for k in range(D // TALL):
        rows_of(k).wait()


def weight_gradients(queries, received):
    vmem = pl.BlockSpec(memory_space=pltpu.VMEM)
    return pl.pallas_call(
        weight_kernel,
        in_specs=[vmem, vmem],
        out_specs=[pl.BlockSpec(memory_space=pl.ANY), vmem],
        out_shape=[
            jax.ShapeDtypeStruct((D, ROWS * D), BF16),
            jax.ShapeDtypeStruct((ROWS, D), BF16),
        ],
        scratch_shapes=[
            pltpu.VMEM((D, ROWS * D), BF16),
            pltpu.SemaphoreType.DMA((D // TALL,)),
        ],
        compiler_params=pltpu.CompilerParams(vmem_limit_bytes=16 << 20),
        cost_estimate=pl.CostEstimate(
            flops=2 * 64 * D * D * 6, bytes_accessed=D * D * 12, transcendentals=0
        ),
        name="weight_gradients",
    )(queries, received)


def sums_kernel(sizes, *refs):
    outs = refs[sum(sizes) :]
    at = 0
    for out, size in zip(outs, sizes):
        total = refs[at][...].astype(F32)
        for term in refs[at + 1 : at + size]:
            total = total + term[...].astype(F32)
        out[...] = total.astype(BF16)
        at += size


def sums(*groups):
    def half_of(h):
        return pl.BlockSpec((DOCS // 4, D), lambda i: (2 * h + i, 0))

    terms = [term for group in groups for term in group]
    return pl.pallas_call(
        functools.partial(sums_kernel, [len(group) for group in groups]),
        grid=(2,),
        in_specs=[half_of(h) for _, h in terms],
        out_specs=[half_of(0) for _ in groups],
        out_shape=[jax.ShapeDtypeStruct((DOCS // 2, D), BF16) for _ in groups],
        compiler_params=pltpu.CompilerParams(vmem_limit_bytes=12 << 20),
        cost_estimate=pl.CostEstimate(
            flops=len(terms) * DOCS * D, bytes_accessed=len(terms) * DOCS * D, transcendentals=0
        ),
    )(*(array for array, _ in terms))


def final_kernel(mine_ref, other_ref, ul_ref, dl_ref, uh_ref, dh_ref, out_ref):
    half = DOCS // 2
    for rows, a, b in ((slice(0, half), ul_ref, dl_ref), (slice(half, DOCS), uh_ref, dh_ref)):
        total = mine_ref[rows].astype(F32) + other_ref[rows].astype(F32)
        total = total + a[...].astype(F32) + b[...].astype(F32)
        out_ref[rows] = total.astype(BF16)


def document_sum(*parts):
    return pl.pallas_call(
        final_kernel,
        out_shape=jax.ShapeDtypeStruct((DOCS, D), BF16),
        compiler_params=pltpu.CompilerParams(vmem_limit_bytes=12 << 20),
        cost_estimate=pl.CostEstimate(
            flops=4 * DOCS * D, bytes_accessed=10 * DOCS * D, transcendentals=0
        ),
        name="document_sum",
    )(*parts)


def up(a):
    return lax.ppermute(a, "z", [(i, (i + 1) % 4) for i in range(4)])


def down(a):
    return lax.ppermute(a, "z", [(i, (i + 3) % 4) for i in range(4)])


def swap(a):
    return lax.ppermute(a, "c", [(0, 1), (1, 0)])


def exchange(a, axes):
    return lax.all_to_all(a, axes, split_axis=0, concat_axis=0, tiled=True)


def step(queries, hyper_weight, hyper_bias, documents, teacher):
    z, c = lax.axis_index("z"), lax.axis_index("c")
    generated, low, high = generate(
        queries, hyper_weight, hyper_bias.T, teacher.T, documents
    )
    below_low = up(low)
    above_high = down(high)
    below_high = up(high)
    above_low = down(low)
    far = (up(below_low), down(above_high))
    docs = []
    for pair in (far, (below_low, below_high), (above_low, above_high)):
        docs += [*pair, swap(pair[0]), swap(pair[1])]
    docs += [documents, swap(documents)]
    pieces = exchange(generated, RING)
    src = jnp.stack(
        [((z + dz) % 4) * 2 + core for dz in (2, 3, 1, 0) for core in (c, 1 - c)]
    ).astype(jnp.int32)
    chunk, targets = assemble(src, pieces)
    gathered = exchange(chunk, PLANE)
    *parts, layer_grad = gradients(targets, gathered, docs)
    arrived = exchange(layer_grad, PLANE)
    pieces = exchange(reduced(arrived), RING)
    far, below, above, own = parts[0::2]
    for_far, for_below, for_above, for_own = (swap(a) for a in parts[1::2])
    first = sums([(far, 0), (for_far, 0)], [(far, 1), (for_far, 1)])
    far_low, far_high = up(first[0]), down(first[1])
    second = sums([(above, 1), (for_above, 1)], [(below, 0), (for_below, 0)])
    up_high, down_low = up(second[0]), down(second[1])
    third = sums(
        [(above, 0), (for_above, 0), (far_low, 0)], [(below, 1), (for_below, 1), (far_high, 0)]
    )
    up_low, down_high = up(third[0]), down(third[1])
    doc_grad = document_sum(own, for_own, up_low, down_low, up_high, down_high)
    weight_grad, bias_grad = weight_gradients(queries, pieces)
    return doc_grad, weight_grad, bias_grad.T


def solution(mesh):
    torus = Mesh(mesh.devices.reshape(2, 2, 4, 4, 2), AXES)
    in_specs = (P(), P(None, AXES), P(None, AXES), P(AXES, None), P(AXES, None))
    out_specs = (P(AXES, None), P(None, AXES), P(None, AXES))
    return jax.shard_map(step, mesh=torus, in_specs=in_specs, out_specs=out_specs, check_vma=False)
```

```python
import functools

import jax
import jax.numpy as jnp
from jax import lax
from jax.experimental import pallas as pl
from jax.experimental.pallas import tpu as pltpu
from jax.sharding import Mesh
from jax.sharding import PartitionSpec as P


AXES = ("xl", "xh", "y", "z", "c")
PLANE = ("xl", "xh", "y")
RING = ("z", "c")
D = 768
Q = 8
ROWS = 6
CHIPS = 16
CHUNK = 48
DOCS = 512
WIRE = 296
TALL = 128
SCALE = D ** (-0.5)
F32 = jnp.float32
BF16 = jnp.bfloat16
TN = (((0,), (0,)), ((), ()))
NT = (((1,), (1,)), ((), ()))
NN = (((1,), (0,)), ((), ()))


def iota(shape, dim):
    return lax.broadcasted_iota(jnp.int32, shape, dim)


def one_hot(cond):
    return jnp.where(cond, 1.0, 0.0).astype(BF16)


def mm(a, b, dims=NN):
    return lax.dot_general(a, b, dims, preferred_element_type=F32)


def gen_kernel(q_ref, w_ref, hb_ref, t_ref, d_ref, out_ref, low_ref, high_ref, wbuf, dbuf, sem):
    def columns(n):
        cols = pl.ds(n * D, D)
        return pltpu.make_async_copy(w_ref.at[:, cols], wbuf.at[:, cols], sem.at[n])

    half = DOCS // 2
    docs_in = pltpu.make_async_copy(d_ref, dbuf, sem.at[ROWS])
    low_out = pltpu.make_async_copy(dbuf.at[0:half], low_ref, sem.at[ROWS + 1])
    high_out = pltpu.make_async_copy(dbuf.at[half:DOCS], high_ref, sem.at[ROWS + 2])
    for n in range(ROWS):
        columns(n).start()
        if n == 2:
            docs_in.start()
    row, col = iota((64, Q), 0), iota((64, Q), 1)
    sub = iota((64, D), 0) % 8
    rep = mm(one_hot(row // 8 == col), q_ref[...])
    placed = jnp.where(sub == 6, rep, 0.0).astype(BF16)
    bias = mm(placed, hb_ref[...], NT)
    targets = mm(one_hot(row == col * 8 + 7), t_ref[...])
    total = jnp.zeros((64, D), F32)
    for n in range(ROWS):
        placed = jnp.where(sub == n, rep, 0.0).astype(BF16)
        columns(n).wait()
        if n == ROWS - 2:
            docs_in.wait()
            low_out.start()
            high_out.start()
        total = total + mm(placed, wbuf[:, n * D : (n + 1) * D])
    out_ref[:, DOCS:] = total[:, DOCS:].astype(BF16)
    total = total[:, 0:DOCS] + targets
    out_ref[:, 128:DOCS] = total[:, 128:].astype(BF16)
    m, l = iota((8, 128), 0), iota((8, 128), 1)
    bias = jnp.concatenate([bias, jnp.zeros((64, 2), F32)], axis=1).astype(BF16)
    bias = mm(bias, one_hot(m == l))
    out_ref[:, 0:128] = (total[:, 0:128] + bias).astype(BF16)
    low_out.wait()
    high_out.wait()


def generate(queries, weight, bias_t, teacher_t, documents):
    hbm = pl.BlockSpec(memory_space=pl.ANY)
    vmem = pl.BlockSpec(memory_space=pltpu.VMEM)
    return pl.pallas_call(
        gen_kernel,
        in_specs=[vmem, hbm, vmem, vmem, hbm],
        out_specs=[vmem, hbm, hbm],
        out_shape=[jax.ShapeDtypeStruct((64, D), BF16)]
        + [jax.ShapeDtypeStruct((DOCS // 2, D), BF16)] * 2,
        scratch_shapes=[
            pltpu.VMEM((D, ROWS * D), BF16),
            pltpu.VMEM((DOCS, D), BF16),
            pltpu.SemaphoreType.DMA((ROWS + 3,)),
        ],
        compiler_params=pltpu.CompilerParams(vmem_limit_bytes=60 << 20),
        cost_estimate=pl.CostEstimate(
            flops=2 * 64 * D * D * 6, bytes_accessed=D * D * 12, transcendentals=0
        ),
        name="generate",
    )(queries, weight, bias_t, teacher_t, documents)


def assemble_kernel(src_ref, r_ref, out_ref, tgt_ref):
    r = r_ref[...]
    a, b = iota((CHUNK, 64), 0), iota((CHUNK, 64), 1)
    rows = mm(one_hot((a // 6 == b // 8) & (a % 6 == b % 8)), r).astype(BF16)
    row, lane = iota((64, 128), 0), iota((64, 128), 1)
    l, m = iota((128, 128), 0), iota((128, 128), 1)
    spread = mm(r[:, 0:128], one_hot((m % 6 == l) & (l < 6) & (m < CHUNK)))
    spread = jnp.where((lane // 6 == row // 8) & (row % 8 == 6), spread, 0.0)
    bias = jnp.sum(spread, axis=0, keepdims=True)
    bias = jnp.where(iota((8, 128), 0) == 0, bias, 0.0).astype(BF16)
    for chip in range(CHIPS):
        for rb in range(3):
            for cb in range(6):
                out_ref[chip, (rb * 6 + cb) * 16 : (rb * 6 + cb + 1) * 16, :] = rows[
                    rb * 16 : (rb + 1) * 16, cb * 128 : (cb + 1) * 128
                ]
        out_ref[chip, 288:296, :] = bias
    row8, col8 = iota((64, 8), 0), iota((64, 8), 1)
    pick = jnp.zeros((64, 8), F32)
    for k in range(8):
        pick = jnp.where((col8 == k) & (row8 == src_ref[k] * 8 + 7), 1.0, pick)
    tgt_ref[...] = mm(r[:, 0:DOCS], pick.astype(BF16), TN)


def assemble(src, received):
    return pl.pallas_call(
        assemble_kernel,
        in_specs=[pl.BlockSpec(memory_space=pltpu.SMEM), pl.BlockSpec(memory_space=pltpu.VMEM)],
        out_specs=[pl.BlockSpec(memory_space=pltpu.VMEM)] * 2,
        out_shape=[
            jax.ShapeDtypeStruct((CHIPS, WIRE, 128), BF16),
            jax.ShapeDtypeStruct((DOCS, 8), F32),
        ],
        compiler_params=pltpu.CompilerParams(vmem_limit_bytes=8 << 20),
        name="assemble",
    )(src, received)


def main_kernel(tgt_ref, g_ref, *refs):
    docs, outs = refs[:14], refs[14:22]
    lg_ref, dbuf, bbuf, pbuf, layer, bacc, even, odd, in_sem, out_sem = refs[22:]
    half = DOCS // 2

    def block(n, size=DOCS):
        return pl.ds(n * size, size)

    for n in range(12):
        pltpu.make_async_copy(docs[n], dbuf.at[block(n, half)], in_sem.at[n // 2]).start()
    for n in range(6, 8):
        pltpu.make_async_copy(docs[n + 6], dbuf.at[block(n)], in_sem.at[n]).start()

    for chip in range(CHIPS):
        for rb in range(3):
            for cb in range(6):
                layer[
                    chip * CHUNK + rb * 16 : chip * CHUNK + (rb + 1) * 16, cb * 128 : (cb + 1) * 128
                ] = g_ref[chip, (rb * 6 + cb) * 16 : (rb * 6 + cb + 1) * 16, :]
    bacc[...] = jnp.zeros_like(bacc)
    chip_row = iota((CHIPS, 128), 0)
    pieces = jnp.zeros((CHIPS, 128), F32)
    for chip in range(CHIPS):
        piece = g_ref[chip, 288:296, :].astype(F32)[0:1, :]
        pieces = jnp.where(chip_row == chip, piece, pieces)
    l, j = iota((128, D), 0), iota((128, D), 1)
    spread = mm(pieces.astype(BF16), one_hot((j % CHUNK == l) & (l < CHUNK)))
    own = iota((CHIPS, D), 1) // CHUNK == iota((CHIPS, D), 0)
    bias = jnp.sum(jnp.where(own, spread, 0.0), axis=0, keepdims=True)

    steps = 8 * DOCS // half
    slots = (even, odd)

    def product(n):
        if n % 2 == 0:
            landed = dbuf.at[block(n // 2)]
            pltpu.make_async_copy(landed, landed, in_sem.at[n // 2]).wait()
        slots[n % 2][...] = mm(dbuf[block(n, half)], layer[...]) + bias

    def errors_of(n):
        preact = slots[n % 2][...]
        tgt = tgt_ref[block(n % 2, half)]
        tgt = jnp.sum(jnp.where(iota((half, 8), 1) == n // 2, tgt, 0.0), axis=1, keepdims=True)
        scores = jnp.sum(jnp.maximum(preact, 0.0), axis=1, keepdims=True) * SCALE
        errors = ((scores - tgt) * SCALE).astype(BF16).astype(F32)
        back = jnp.where(preact > 0, errors, 0.0)
        bbuf[block(n, half)] = back.astype(BF16)
        bacc[...] += jnp.sum(back.reshape(-1, 8, D), axis=0)

    product(0)
    for n in range(steps):
        if n + 1 < steps:
            product(n + 1)
        errors_of(n)

    for n in range(2):
        rows = block(n, 4 * DOCS)
        pbuf[rows] = mm(bbuf[rows], layer[...], NT).astype(BF16)
        for k in range(4 * n, 4 * n + 4):
            pltpu.make_async_copy(pbuf.at[block(k)], outs[k], out_sem.at[k]).start()

    grad = mm(dbuf[...], bbuf[...], TN).astype(BF16)
    for chip in range(CHIPS):
        for rb in range(3):
            rows = slice(chip * CHUNK + rb * 16, chip * CHUNK + (rb + 1) * 16)
            for cb in range(6):
                lg_ref[chip, (rb * 6 + cb) * 16 : (rb * 6 + cb + 1) * 16, :] = grad[
                    rows, cb * 128 : (cb + 1) * 128
                ]
    total = jnp.sum(bacc[...], axis=0, keepdims=True)
    high = total.astype(BF16)
    low = (total - high.astype(F32)).astype(BF16)
    j, l = iota((D, 128), 0), iota((D, 128), 1)
    fold = one_hot((j % CHUNK == l) & (l < CHUNK))
    high = mm(jnp.where(own, high.astype(F32), 0.0).astype(BF16), fold)
    low = mm(jnp.where(own, low.astype(F32), 0.0).astype(BF16), fold)
    sub = iota((8, 128), 0)
    for chip in range(CHIPS):
        tile = jnp.where(sub == 0, high[chip : chip + 1], jnp.where(sub == 1, low[chip : chip + 1], 0.0))
        lg_ref[chip, 288:296, :] = tile.astype(BF16)
    for n in range(8):
        pltpu.make_async_copy(pbuf.at[block(n)], outs[n], out_sem.at[n]).wait()


def gradients(tgt, gathered, docs):
    hbm = pl.BlockSpec(memory_space=pl.ANY)
    vmem = pl.BlockSpec(memory_space=pltpu.VMEM)
    return pl.pallas_call(
        main_kernel,
        in_specs=[vmem, vmem] + [hbm] * 14,
        out_specs=[hbm] * 8 + [vmem],
        out_shape=[jax.ShapeDtypeStruct((DOCS, D), BF16)] * 8
        + [jax.ShapeDtypeStruct((CHIPS, WIRE, 128), BF16)],
        scratch_shapes=[pltpu.VMEM((8 * DOCS, D), BF16)] * 3
        + [
            pltpu.VMEM((D, D), BF16),
            pltpu.VMEM((8, D), F32),
            pltpu.VMEM((DOCS // 2, D), F32),
            pltpu.VMEM((DOCS // 2, D), F32),
            pltpu.SemaphoreType.DMA((8,)),
            pltpu.SemaphoreType.DMA((8,)),
        ],
        compiler_params=pltpu.CompilerParams(vmem_limit_bytes=51 << 20),
        cost_estimate=pl.CostEstimate(
            flops=6 * 8 * DOCS * D * D, bytes_accessed=32 * DOCS * D, transcendentals=0
        ),
        name="gradients",
    )(tgt, gathered, *docs)


def reduce_kernel(y_ref, out_ref):
    total = y_ref[0].astype(F32)
    for chip in range(1, CHIPS):
        total = total + y_ref[chip].astype(F32)
    rows = jnp.concatenate(
        [
            jnp.concatenate(
                [total[(rb * 6 + cb) * 16 : (rb * 6 + cb + 1) * 16] for cb in range(6)], axis=1
            )
            for rb in range(3)
        ],
        axis=0,
    ).astype(BF16)
    a, b = iota((64, CHUNK), 0), iota((64, CHUNK), 1)
    pieces = mm(one_hot((b // 6 == a // 8) & (b % 6 == a % 8)), rows)
    bias = jnp.sum(total[288:296], axis=0, keepdims=True).astype(BF16).astype(F32)
    row, lane = iota((64, 128), 0), iota((64, 128), 1)
    mine = jnp.where((lane // 6 == row // 8) & (row % 8 == 6) & (lane < CHUNK), bias, 0.0)
    m, l = iota((128, 128), 0), iota((128, 128), 1)
    bias = mm(mine.astype(BF16), one_hot((m % 6 == l) & (l < 6) & (m < CHUNK)))
    out_ref[:, 0:128] = (pieces[:, 0:128] + bias).astype(BF16)
    out_ref[:, 128:] = pieces[:, 128:].astype(BF16)


def reduced(arrived):
    return pl.pallas_call(
        reduce_kernel,
        out_shape=jax.ShapeDtypeStruct((64, D), BF16),
        compiler_params=pltpu.CompilerParams(vmem_limit_bytes=8 << 20),
        name="reduced",
    )(arrived)


def weight_kernel(q_ref, r_ref, out_ref, bias_ref, obuf, sem):
    def rows_of(n):
        rows = pl.ds(n * TALL, TALL)
        return pltpu.make_async_copy(obuf.at[rows], out_ref.at[rows], sem.at[n])

    row, col = iota((64, Q), 0), iota((64, Q), 1)
    sub = iota((64, D), 0) % 8
    rep = mm(one_hot(row // 8 == col), q_ref[...])
    placed = [jnp.where(sub == n, rep, 0.0).astype(BF16) for n in range(7)]
    for k in range(D // TALL):
        rows = slice(k * TALL, (k + 1) * TALL)
        for n in range(ROWS):
            obuf[rows, n * D : (n + 1) * D] = mm(placed[n][:, rows], r_ref[...], TN).astype(BF16)
        rows_of(k).start()
    bias_ref[...] = mm(r_ref[:, 0:128], placed[6], TN)[0:ROWS].astype(BF16)
    for k in range(D // TALL):
        rows_of(k).wait()


def weight_gradients(queries, received):
    vmem = pl.BlockSpec(memory_space=pltpu.VMEM)
    return pl.pallas_call(
        weight_kernel,
        in_specs=[vmem, vmem],
        out_specs=[pl.BlockSpec(memory_space=pl.ANY), vmem],
        out_shape=[
            jax.ShapeDtypeStruct((D, ROWS * D), BF16),
            jax.ShapeDtypeStruct((ROWS, D), BF16),
        ],
        scratch_shapes=[
            pltpu.VMEM((D, ROWS * D), BF16),
            pltpu.SemaphoreType.DMA((D // TALL,)),
        ],
        compiler_params=pltpu.CompilerParams(vmem_limit_bytes=16 << 20),
        cost_estimate=pl.CostEstimate(
            flops=2 * 64 * D * D * 6, bytes_accessed=D * D * 12, transcendentals=0
        ),
        name="weight_gradients",
    )(queries, received)


def sums_kernel(sizes, *refs):
    outs = refs[sum(sizes) :]
    at = 0
    for out, size in zip(outs, sizes):
        total = refs[at][...].astype(F32)
        for term in refs[at + 1 : at + size]:
            total = total + term[...].astype(F32)
        out[...] = total.astype(BF16)
        at += size


def sums(*groups):
    def half_of(h):
        return pl.BlockSpec((DOCS // 4, D), lambda i: (2 * h + i, 0))

    terms = [term for group in groups for term in group]
    return pl.pallas_call(
        functools.partial(sums_kernel, [len(group) for group in groups]),
        grid=(2,),
        in_specs=[half_of(h) for _, h in terms],
        out_specs=[half_of(0) for _ in groups],
        out_shape=[jax.ShapeDtypeStruct((DOCS // 2, D), BF16) for _ in groups],
        compiler_params=pltpu.CompilerParams(vmem_limit_bytes=12 << 20),
        cost_estimate=pl.CostEstimate(
            flops=len(terms) * DOCS * D, bytes_accessed=len(terms) * DOCS * D, transcendentals=0
        ),
    )(*(array for array, _ in terms))


def final_kernel(mine_ref, other_ref, ul_ref, dl_ref, uh_ref, dh_ref, out_ref):
    half = DOCS // 2
    for rows, a, b in ((slice(0, half), ul_ref, dl_ref), (slice(half, DOCS), uh_ref, dh_ref)):
        total = mine_ref[rows].astype(F32) + other_ref[rows].astype(F32)
        total = total + a[...].astype(F32) + b[...].astype(F32)
        out_ref[rows] = total.astype(BF16)


def document_sum(*parts):
    return pl.pallas_call(
        final_kernel,
        out_shape=jax.ShapeDtypeStruct((DOCS, D), BF16),
        compiler_params=pltpu.CompilerParams(vmem_limit_bytes=12 << 20),
        cost_estimate=pl.CostEstimate(
            flops=4 * DOCS * D, bytes_accessed=10 * DOCS * D, transcendentals=0
        ),
        name="document_sum",
    )(*parts)


def up(a):
    return lax.ppermute(a, "z", [(i, (i + 1) % 4) for i in range(4)])


def down(a):
    return lax.ppermute(a, "z", [(i, (i + 3) % 4) for i in range(4)])


def swap(a):
    return lax.ppermute(a, "c", [(0, 1), (1, 0)])


def exchange(a, axes):
    return lax.all_to_all(a, axes, split_axis=0, concat_axis=0, tiled=True)


def step(queries, hyper_weight, hyper_bias, documents, teacher):
    z, c = lax.axis_index("z"), lax.axis_index("c")
    generated, low, high = generate(
        queries, hyper_weight, hyper_bias.T, teacher.T, documents
    )
    below_low = up(low)
    above_high = down(high)
    below_high = up(high)
    above_low = down(low)
    far = (up(below_low), down(above_high))
    docs = []
    for pair in (far, (below_low, below_high), (above_low, above_high)):
        docs += [*pair, swap(pair[0]), swap(pair[1])]
    docs += [documents, swap(documents)]
    pieces = exchange(generated, RING)
    src = jnp.stack(
        [((z + dz) % 4) * 2 + core for dz in (2, 3, 1, 0) for core in (c, 1 - c)]
    ).astype(jnp.int32)
    chunk, targets = assemble(src, pieces)
    gathered = exchange(chunk, PLANE)
    *parts, layer_grad = gradients(targets, gathered, docs)
    arrived = exchange(layer_grad, PLANE)
    pieces = exchange(reduced(arrived), RING)
    far, below, above, own = parts[0::2]
    for_far, for_below, for_above, for_own = (swap(a) for a in parts[1::2])
    first = sums([(far, 0), (for_far, 0)], [(far, 1), (for_far, 1)])
    far_low, far_high = up(first[0]), down(first[1])
    second = sums([(above, 1), (for_above, 1)], [(below, 0), (for_below, 0)])
    up_high, down_low = up(second[0]), down(second[1])
    third = sums(
        [(above, 0), (for_above, 0), (far_low, 0)], [(below, 1), (for_below, 1), (far_high, 0)]
    )
    up_low, down_high = up(third[0]), down(third[1])
    doc_grad = document_sum(own, for_own, up_low, down_low, up_high, down_high)
    weight_grad, bias_grad = weight_gradients(queries, pieces)
    return doc_grad, weight_grad, bias_grad.T


def solution(mesh):
    torus = Mesh(mesh.devices.reshape(2, 2, 4, 4, 2), AXES)
    in_specs = (P(), P(None, AXES), P(None, AXES), P(AXES, None), P(AXES, None))
    out_specs = (P(AXES, None), P(None, AXES), P(None, AXES))
    return jax.shard_map(step, mesh=torus, in_specs=in_specs, out_specs=out_specs, check_vma=False)
```

```python
import functools

import jax
import jax.numpy as jnp
from jax import lax
from jax.experimental import pallas as pl
from jax.experimental.pallas import tpu as pltpu
from jax.sharding import Mesh
from jax.sharding import PartitionSpec as P


AXES = ("xl", "xh", "y", "z", "c")
PLANE = ("xl", "xh", "y")
RING = ("z", "c")
D = 768
Q = 8
ROWS = 6
CHIPS = 16
CHUNK = 48
DOCS = 512
WIRE = 296
TALL = 128
SCALE = D ** (-0.5)
F32 = jnp.float32
BF16 = jnp.bfloat16
TN = (((0,), (0,)), ((), ()))
NT = (((1,), (1,)), ((), ()))
NN = (((1,), (0,)), ((), ()))


def iota(shape, dim):
    return lax.broadcasted_iota(jnp.int32, shape, dim)


def one_hot(cond):
    return jnp.where(cond, 1.0, 0.0).astype(BF16)


def mm(a, b, dims=NN):
    return lax.dot_general(a, b, dims, preferred_element_type=F32)


def gen_kernel(q_ref, w_ref, hb_ref, t_ref, d_ref, out_ref, low_ref, high_ref, wbuf, dbuf, sem):
    def columns(n):
        cols = pl.ds(n * D, D)
        return pltpu.make_async_copy(w_ref.at[:, cols], wbuf.at[:, cols], sem.at[n])

    half = DOCS // 2
    docs_in = pltpu.make_async_copy(d_ref, dbuf, sem.at[ROWS])
    low_out = pltpu.make_async_copy(dbuf.at[0:half], low_ref, sem.at[ROWS + 1])
    high_out = pltpu.make_async_copy(dbuf.at[half:DOCS], high_ref, sem.at[ROWS + 2])
    for n in range(ROWS):
        columns(n).start()
        if n == 2:
            docs_in.start()
    row, col = iota((64, Q), 0), iota((64, Q), 1)
    sub = iota((64, D), 0) % 8
    rep = mm(one_hot(row // 8 == col), q_ref[...])
    placed = jnp.where(sub == 6, rep, 0.0).astype(BF16)
    bias = mm(placed, hb_ref[...], NT)
    targets = mm(one_hot(row == col * 8 + 7), t_ref[...])
    total = jnp.zeros((64, D), F32)
    for n in range(ROWS):
        placed = jnp.where(sub == n, rep, 0.0).astype(BF16)
        columns(n).wait()
        if n == ROWS - 2:
            docs_in.wait()
            low_out.start()
            high_out.start()
        total = total + mm(placed, wbuf[:, n * D : (n + 1) * D])
    out_ref[:, DOCS:] = total[:, DOCS:].astype(BF16)
    total = total[:, 0:DOCS] + targets
    out_ref[:, 128:DOCS] = total[:, 128:].astype(BF16)
    m, l = iota((8, 128), 0), iota((8, 128), 1)
    bias = jnp.concatenate([bias, jnp.zeros((64, 2), F32)], axis=1).astype(BF16)
    bias = mm(bias, one_hot(m == l))
    out_ref[:, 0:128] = (total[:, 0:128] + bias).astype(BF16)
    low_out.wait()
    high_out.wait()


def generate(queries, weight, bias_t, teacher_t, documents):
    hbm = pl.BlockSpec(memory_space=pl.ANY)
    vmem = pl.BlockSpec(memory_space=pltpu.VMEM)
    return pl.pallas_call(
        gen_kernel,
        in_specs=[vmem, hbm, vmem, vmem, hbm],
        out_specs=[vmem, hbm, hbm],
        out_shape=[jax.ShapeDtypeStruct((64, D), BF16)]
        + [jax.ShapeDtypeStruct((DOCS // 2, D), BF16)] * 2,
        scratch_shapes=[
            pltpu.VMEM((D, ROWS * D), BF16),
            pltpu.VMEM((DOCS, D), BF16),
            pltpu.SemaphoreType.DMA((ROWS + 3,)),
        ],
        compiler_params=pltpu.CompilerParams(vmem_limit_bytes=60 << 20),
        cost_estimate=pl.CostEstimate(
            flops=2 * 64 * D * D * 6, bytes_accessed=D * D * 12, transcendentals=0
        ),
        name="generate",
    )(queries, weight, bias_t, teacher_t, documents)


def assemble_kernel(src_ref, r_ref, out_ref, tgt_ref):
    r = r_ref[...]
    a, b = iota((CHUNK, 64), 0), iota((CHUNK, 64), 1)
    rows = mm(one_hot((a // 6 == b // 8) & (a % 6 == b % 8)), r).astype(BF16)
    row, lane = iota((64, 128), 0), iota((64, 128), 1)
    l, m = iota((128, 128), 0), iota((128, 128), 1)
    spread = mm(r[:, 0:128], one_hot((m % 6 == l) & (l < 6) & (m < CHUNK)))
    spread = jnp.where((lane // 6 == row // 8) & (row % 8 == 6), spread, 0.0)
    bias = jnp.sum(spread, axis=0, keepdims=True)
    bias = jnp.where(iota((8, 128), 0) == 0, bias, 0.0).astype(BF16)
    for chip in range(CHIPS):
        for rb in range(3):
            for cb in range(6):
                out_ref[chip, (rb * 6 + cb) * 16 : (rb * 6 + cb + 1) * 16, :] = rows[
                    rb * 16 : (rb + 1) * 16, cb * 128 : (cb + 1) * 128
                ]
        out_ref[chip, 288:296, :] = bias
    row8, col8 = iota((64, 8), 0), iota((64, 8), 1)
    pick = jnp.zeros((64, 8), F32)
    for k in range(8):
        pick = jnp.where((col8 == k) & (row8 == src_ref[k] * 8 + 7), 1.0, pick)
    tgt_ref[...] = mm(r[:, 0:DOCS], pick.astype(BF16), TN)


def assemble(src, received):
    return pl.pallas_call(
        assemble_kernel,
        in_specs=[pl.BlockSpec(memory_space=pltpu.SMEM), pl.BlockSpec(memory_space=pltpu.VMEM)],
        out_specs=[pl.BlockSpec(memory_space=pltpu.VMEM)] * 2,
        out_shape=[
            jax.ShapeDtypeStruct((CHIPS, WIRE, 128), BF16),
            jax.ShapeDtypeStruct((DOCS, 8), F32),
        ],
        compiler_params=pltpu.CompilerParams(vmem_limit_bytes=8 << 20),
        name="assemble",
    )(src, received)


def main_kernel(tgt_ref, g_ref, *refs):
    docs, outs = refs[:14], refs[14:22]
    lg_ref, dbuf, bbuf, pbuf, layer, bacc, even, odd, in_sem, out_sem = refs[22:]
    half = DOCS // 2

    def block(n, size=DOCS):
        return pl.ds(n * size, size)

    for n in range(12):
        pltpu.make_async_copy(docs[n], dbuf.at[block(n, half)], in_sem.at[n // 2]).start()
    for n in range(6, 8):
        pltpu.make_async_copy(docs[n + 6], dbuf.at[block(n)], in_sem.at[n]).start()

    for chip in range(CHIPS):
        for rb in range(3):
            for cb in range(6):
                layer[
                    chip * CHUNK + rb * 16 : chip * CHUNK + (rb + 1) * 16, cb * 128 : (cb + 1) * 128
                ] = g_ref[chip, (rb * 6 + cb) * 16 : (rb * 6 + cb + 1) * 16, :]
    bacc[...] = jnp.zeros_like(bacc)
    chip_row = iota((CHIPS, 128), 0)
    pieces = jnp.zeros((CHIPS, 128), F32)
    for chip in range(CHIPS):
        piece = g_ref[chip, 288:296, :].astype(F32)[0:1, :]
        pieces = jnp.where(chip_row == chip, piece, pieces)
    l, j = iota((128, D), 0), iota((128, D), 1)
    spread = mm(pieces.astype(BF16), one_hot((j % CHUNK == l) & (l < CHUNK)))
    own = iota((CHIPS, D), 1) // CHUNK == iota((CHIPS, D), 0)
    bias = jnp.sum(jnp.where(own, spread, 0.0), axis=0, keepdims=True)

    steps = 8 * DOCS // half
    slots = (even, odd)

    def product(n):
        if n % 2 == 0:
            landed = dbuf.at[block(n // 2)]
            pltpu.make_async_copy(landed, landed, in_sem.at[n // 2]).wait()
        slots[n % 2][...] = mm(dbuf[block(n, half)], layer[...]) + bias

    def errors_of(n):
        preact = slots[n % 2][...]
        tgt = tgt_ref[block(n % 2, half)]
        tgt = jnp.sum(jnp.where(iota((half, 8), 1) == n // 2, tgt, 0.0), axis=1, keepdims=True)
        scores = jnp.sum(jnp.maximum(preact, 0.0), axis=1, keepdims=True) * SCALE
        errors = ((scores - tgt) * SCALE).astype(BF16).astype(F32)
        back = jnp.where(preact > 0, errors, 0.0)
        bbuf[block(n, half)] = back.astype(BF16)
        bacc[...] += jnp.sum(back.reshape(-1, 8, D), axis=0)

    product(0)
    product(1)
    for n in range(steps):
        errors_of(n)
        if n + 2 < steps:
            product(n + 2)

    for n in range(2):
        rows = block(n, 4 * DOCS)
        pbuf[rows] = mm(bbuf[rows], layer[...], NT).astype(BF16)
        for k in range(4 * n, 4 * n + 4):
            pltpu.make_async_copy(pbuf.at[block(k)], outs[k], out_sem.at[k]).start()

    grad = mm(dbuf[...], bbuf[...], TN).astype(BF16)
    for chip in range(CHIPS):
        for rb in range(3):
            rows = slice(chip * CHUNK + rb * 16, chip * CHUNK + (rb + 1) * 16)
            for cb in range(6):
                lg_ref[chip, (rb * 6 + cb) * 16 : (rb * 6 + cb + 1) * 16, :] = grad[
                    rows, cb * 128 : (cb + 1) * 128
                ]
    total = jnp.sum(bacc[...], axis=0, keepdims=True)
    high = total.astype(BF16)
    low = (total - high.astype(F32)).astype(BF16)
    j, l = iota((D, 128), 0), iota((D, 128), 1)
    fold = one_hot((j % CHUNK == l) & (l < CHUNK))
    high = mm(jnp.where(own, high.astype(F32), 0.0).astype(BF16), fold)
    low = mm(jnp.where(own, low.astype(F32), 0.0).astype(BF16), fold)
    sub = iota((8, 128), 0)
    for chip in range(CHIPS):
        tile = jnp.where(sub == 0, high[chip : chip + 1], jnp.where(sub == 1, low[chip : chip + 1], 0.0))
        lg_ref[chip, 288:296, :] = tile.astype(BF16)
    for n in range(8):
        pltpu.make_async_copy(pbuf.at[block(n)], outs[n], out_sem.at[n]).wait()


def gradients(tgt, gathered, docs):
    hbm = pl.BlockSpec(memory_space=pl.ANY)
    vmem = pl.BlockSpec(memory_space=pltpu.VMEM)
    return pl.pallas_call(
        main_kernel,
        in_specs=[vmem, vmem] + [hbm] * 14,
        out_specs=[hbm] * 8 + [vmem],
        out_shape=[jax.ShapeDtypeStruct((DOCS, D), BF16)] * 8
        + [jax.ShapeDtypeStruct((CHIPS, WIRE, 128), BF16)],
        scratch_shapes=[pltpu.VMEM((8 * DOCS, D), BF16)] * 3
        + [
            pltpu.VMEM((D, D), BF16),
            pltpu.VMEM((8, D), F32),
            pltpu.VMEM((DOCS // 2, D), F32),
            pltpu.VMEM((DOCS // 2, D), F32),
            pltpu.SemaphoreType.DMA((8,)),
            pltpu.SemaphoreType.DMA((8,)),
        ],
        compiler_params=pltpu.CompilerParams(vmem_limit_bytes=51 << 20),
        cost_estimate=pl.CostEstimate(
            flops=6 * 8 * DOCS * D * D, bytes_accessed=32 * DOCS * D, transcendentals=0
        ),
        name="gradients",
    )(tgt, gathered, *docs)


def reduce_kernel(y_ref, out_ref):
    total = y_ref[0].astype(F32)
    for chip in range(1, CHIPS):
        total = total + y_ref[chip].astype(F32)
    rows = jnp.concatenate(
        [
            jnp.concatenate(
                [total[(rb * 6 + cb) * 16 : (rb * 6 + cb + 1) * 16] for cb in range(6)], axis=1
            )
            for rb in range(3)
        ],
        axis=0,
    ).astype(BF16)
    a, b = iota((64, CHUNK), 0), iota((64, CHUNK), 1)
    pieces = mm(one_hot((b // 6 == a // 8) & (b % 6 == a % 8)), rows)
    bias = jnp.sum(total[288:296], axis=0, keepdims=True).astype(BF16).astype(F32)
    row, lane = iota((64, 128), 0), iota((64, 128), 1)
    mine = jnp.where((lane // 6 == row // 8) & (row % 8 == 6) & (lane < CHUNK), bias, 0.0)
    m, l = iota((128, 128), 0), iota((128, 128), 1)
    bias = mm(mine.astype(BF16), one_hot((m % 6 == l) & (l < 6) & (m < CHUNK)))
    out_ref[:, 0:128] = (pieces[:, 0:128] + bias).astype(BF16)
    out_ref[:, 128:] = pieces[:, 128:].astype(BF16)


def reduced(arrived):
    return pl.pallas_call(
        reduce_kernel,
        out_shape=jax.ShapeDtypeStruct((64, D), BF16),
        compiler_params=pltpu.CompilerParams(vmem_limit_bytes=8 << 20),
        name="reduced",
    )(arrived)


def weight_kernel(q_ref, r_ref, out_ref, bias_ref, obuf, sem):
    def rows_of(n):
        rows = pl.ds(n * TALL, TALL)
        return pltpu.make_async_copy(obuf.at[rows], out_ref.at[rows], sem.at[n])

    row, col = iota((64, Q), 0), iota((64, Q), 1)
    sub = iota((64, D), 0) % 8
    rep = mm(one_hot(row // 8 == col), q_ref[...])
    placed = [jnp.where(sub == n, rep, 0.0).astype(BF16) for n in range(7)]
    for k in range(D // TALL):
        rows = slice(k * TALL, (k + 1) * TALL)
        for n in range(ROWS):
            obuf[rows, n * D : (n + 1) * D] = mm(placed[n][:, rows], r_ref[...], TN).astype(BF16)
        rows_of(k).start()
    bias_ref[...] = mm(r_ref[:, 0:128], placed[6], TN)[0:ROWS].astype(BF16)
    for k in range(D // TALL):
        rows_of(k).wait()


def weight_gradients(queries, received):
    vmem = pl.BlockSpec(memory_space=pltpu.VMEM)
    return pl.pallas_call(
        weight_kernel,
        in_specs=[vmem, vmem],
        out_specs=[pl.BlockSpec(memory_space=pl.ANY), vmem],
        out_shape=[
            jax.ShapeDtypeStruct((D, ROWS * D), BF16),
            jax.ShapeDtypeStruct((ROWS, D), BF16),
        ],
        scratch_shapes=[
            pltpu.VMEM((D, ROWS * D), BF16),
            pltpu.SemaphoreType.DMA((D // TALL,)),
        ],
        compiler_params=pltpu.CompilerParams(vmem_limit_bytes=16 << 20),
        cost_estimate=pl.CostEstimate(
            flops=2 * 64 * D * D * 6, bytes_accessed=D * D * 12, transcendentals=0
        ),
        name="weight_gradients",
    )(queries, received)


def sums_kernel(sizes, *refs):
    outs = refs[sum(sizes) :]
    at = 0
    for out, size in zip(outs, sizes):
        total = refs[at][...].astype(F32)
        for term in refs[at + 1 : at + size]:
            total = total + term[...].astype(F32)
        out[...] = total.astype(BF16)
        at += size


def sums(*groups):
    def half_of(h):
        return pl.BlockSpec((DOCS // 4, D), lambda i: (2 * h + i, 0))

    terms = [term for group in groups for term in group]
    return pl.pallas_call(
        functools.partial(sums_kernel, [len(group) for group in groups]),
        grid=(2,),
        in_specs=[half_of(h) for _, h in terms],
        out_specs=[half_of(0) for _ in groups],
        out_shape=[jax.ShapeDtypeStruct((DOCS // 2, D), BF16) for _ in groups],
        compiler_params=pltpu.CompilerParams(vmem_limit_bytes=12 << 20),
        cost_estimate=pl.CostEstimate(
            flops=len(terms) * DOCS * D, bytes_accessed=len(terms) * DOCS * D, transcendentals=0
        ),
    )(*(array for array, _ in terms))


def final_kernel(mine_ref, other_ref, ul_ref, dl_ref, uh_ref, dh_ref, out_ref):
    half = DOCS // 2
    for rows, a, b in ((slice(0, half), ul_ref, dl_ref), (slice(half, DOCS), uh_ref, dh_ref)):
        total = mine_ref[rows].astype(F32) + other_ref[rows].astype(F32)
        total = total + a[...].astype(F32) + b[...].astype(F32)
        out_ref[rows] = total.astype(BF16)


def document_sum(*parts):
    return pl.pallas_call(
        final_kernel,
        out_shape=jax.ShapeDtypeStruct((DOCS, D), BF16),
        compiler_params=pltpu.CompilerParams(vmem_limit_bytes=12 << 20),
        cost_estimate=pl.CostEstimate(
            flops=4 * DOCS * D, bytes_accessed=10 * DOCS * D, transcendentals=0
        ),
        name="document_sum",
    )(*parts)


def up(a):
    return lax.ppermute(a, "z", [(i, (i + 1) % 4) for i in range(4)])


def down(a):
    return lax.ppermute(a, "z", [(i, (i + 3) % 4) for i in range(4)])


def swap(a):
    return lax.ppermute(a, "c", [(0, 1), (1, 0)])


def exchange(a, axes):
    return lax.all_to_all(a, axes, split_axis=0, concat_axis=0, tiled=True)


def step(queries, hyper_weight, hyper_bias, documents, teacher):
    z, c = lax.axis_index("z"), lax.axis_index("c")
    generated, low, high = generate(
        queries, hyper_weight, hyper_bias.T, teacher.T, documents
    )
    below_low = up(low)
    above_high = down(high)
    below_high = up(high)
    above_low = down(low)
    far = (up(below_low), down(above_high))
    docs = []
    for pair in (far, (below_low, below_high), (above_low, above_high)):
        docs += [*pair, swap(pair[0]), swap(pair[1])]
    docs += [documents, swap(documents)]
    pieces = exchange(generated, RING)
    src = jnp.stack(
        [((z + dz) % 4) * 2 + core for dz in (2, 3, 1, 0) for core in (c, 1 - c)]
    ).astype(jnp.int32)
    chunk, targets = assemble(src, pieces)
    gathered = exchange(chunk, PLANE)
    *parts, layer_grad = gradients(targets, gathered, docs)
    arrived = exchange(layer_grad, PLANE)
    pieces = exchange(reduced(arrived), RING)
    far, below, above, own = parts[0::2]
    for_far, for_below, for_above, for_own = (swap(a) for a in parts[1::2])
    first = sums([(far, 0), (for_far, 0)], [(far, 1), (for_far, 1)])
    far_low, far_high = up(first[0]), down(first[1])
    second = sums([(above, 1), (for_above, 1)], [(below, 0), (for_below, 0)])
    up_high, down_low = up(second[0]), down(second[1])
    third = sums(
        [(above, 0), (for_above, 0), (far_low, 0)], [(below, 1), (for_below, 1), (far_high, 0)]
    )
    up_low, down_high = up(third[0]), down(third[1])
    doc_grad = document_sum(own, for_own, up_low, down_low, up_high, down_high)
    weight_grad, bias_grad = weight_gradients(queries, pieces)
    return doc_grad, weight_grad, bias_grad.T


def solution(mesh):
    torus = Mesh(mesh.devices.reshape(2, 2, 4, 4, 2), AXES)
    in_specs = (P(), P(None, AXES), P(None, AXES), P(AXES, None), P(AXES, None))
    out_specs = (P(AXES, None), P(None, AXES), P(None, AXES))
    return jax.shard_map(step, mesh=torus, in_specs=in_specs, out_specs=out_specs, check_vma=False)
```
